512 devices in a mesh: team: 16 (over y, core), tm: 32 (over x, z).
Axes of the slice: x: 4, y: 8, z: 8, core: 2. Of those that a mesh axis runs over, the one named last changes fastest.
Arguments:
- transitions: float32 [16, 32, 512, 512], P('team', 'tm'), may hold values from -0.25 to 1.25
- states: float32 [16, 32, 64, 512], P('team', 'tm'), may hold values from -1 to 1
- cotangent: float32 [16, 32, 64, 512], P('team', 'tm'), may hold values from -2.4 to 2.4
- terminal: float32 [16, 64, 512], P('team'), may hold values from -6 to 6
- incidence: int32 [16, 32, 32, 2048], P('team', 'tm'), may hold values 0 or 1
- measured: float32 [16, 32, 64, 32], P('team', 'tm'), may hold values from -0.12 to 0.12
- obs_gain: float32 [16, 512], P('team'), may hold values from -6 to 6
Outputs:
- adjoint: float32 [16, 32, 64, 512], P('team', 'tm')
- grad_transitions: bfloat16 [16, 32, 512, 512], P('team', 'tm')
The draws below stay inside these ranges and needn't reach their ends.
All inputs are finite; a program needn't handle non-finite values. No bound on the sum of `incidence` on one device may be relied on, other than what follows from the above.
Results may differ from the reference program's by a relative error of at most 0.001.
Values sent between devices are 32-bit elements; how exact they have to be, the bound alone decides.
No kernel may reach another device: no remote copies, remote signals or barrier semaphores. Data moves between devices by JAX's collectives and lax.ppermute only.
A program may use at most 64 MiB of HBM per device.

```python
import math
import jax
import jax.numpy as jnp
from jax import lax

ROBOTS = 32
STATES = 16
TEAM_STATES = 512
COLS = 64
LMK = 2048
ROBOT_TEAMS = 16
WINDOW_STEPS = 32


def draw_transitions(key, part):
    random_keys = jax.random.split(key, 4)
    full_shape = (ROBOT_TEAMS, WINDOW_STEPS, TEAM_STATES, TEAM_STATES)
    noise = jnp.clip(jax.random.normal(random_keys[0], full_shape, jnp.float32), -4.0, 4.0)
    rate_low = 0.8
    spread = 0.3
    baseline_rate = jnp.exp(jax.random.uniform(random_keys[1], (ROBOT_TEAMS, 1, TEAM_STATES), jnp.float32, math.log(rate_low), math.log(0.995)))
    spike_event = jax.random.randint(random_keys[2], (ROBOT_TEAMS, WINDOW_STEPS, TEAM_STATES), 0, 32) == 0
    spike_factor = jnp.where(spike_event, jax.random.uniform(random_keys[3], (ROBOT_TEAMS, WINDOW_STEPS, TEAM_STATES), jnp.float32, 0.5, 0.8), 1.0)
    diagonal_part = baseline_rate * spike_factor
    unit_matrix = jnp.eye(TEAM_STATES, dtype=jnp.float32)
    return noise * (spread / math.sqrt(TEAM_STATES)) + diagonal_part[..., None] * unit_matrix


def with_ends(array, own_key, smallest, high):
    index_at = [jax.random.randint(jax.random.fold_in(own_key, axis), (), 0, length) for axis, length in enumerate(array.shape)]
    widest = array.shape.index(max(array.shape))
    beside = index_at[:widest] + [(index_at[widest] + 1) % array.shape[widest]] + index_at[widest + 1:]
    return array.at[tuple(index_at)].set(smallest).at[tuple(beside)].set(high)


def block_scale(rng, extent, cuts, smallest, largest):
    gain = 1.0
    for position, shards_of in cuts:
        heights = jax.random.uniform(jax.random.fold_in(jax.random.fold_in(rng, 6), position), (shards_of,), jnp.float32, smallest / len(cuts), largest / len(cuts))
        gain = gain * jnp.repeat(jnp.exp(heights), extent[position] // shards_of).reshape((-1,) + (1,) * (len(extent) - 1 - position))
    return gain


def centred(rng, dims, scale, reach, cuts=(), kind=jnp.bfloat16):
    array = jax.random.normal(rng, dims, jnp.float32) * scale
    if len(cuts) > 0:
        array = block_scale(rng, dims, cuts, -0.22, 0.18) * array
    return jnp.clip(array, min=-reach, max=reach).astype(kind)


def setup_inputs(seed: int = 0) -> dict:
    keys = jax.random.split(jax.random.key(seed), 8)
    return {
        "transitions": draw_transitions(jax.random.fold_in(keys[7], 71), 0),
        "states": centred(keys[1], (ROBOT_TEAMS, WINDOW_STEPS, COLS, TEAM_STATES), 0.125, 1.0, ((0, 16), (1, 32)), jnp.float32),
        "cotangent": centred(keys[2], (ROBOT_TEAMS, WINDOW_STEPS, COLS, TEAM_STATES), 0.3, 2.4, ((0, 16), (1, 32)), jnp.float32),
        "terminal": centred(keys[3], (ROBOT_TEAMS, COLS, TEAM_STATES), 1.0, 6.0, ((0, 16),), jnp.float32),
        "incidence": with_ends((jax.random.randint(keys[4], (ROBOT_TEAMS, WINDOW_STEPS, ROBOTS, LMK), 0, LMK) < 64).astype(jnp.int32), jax.random.fold_in(keys[4], 1), 0, 1),
        "measured": centred(keys[5], (ROBOT_TEAMS, WINDOW_STEPS, COLS, ROBOTS), 0.015, 0.12, ((0, 16), (1, 32)), jnp.float32),
        "obs_gain": centred(keys[6], (ROBOT_TEAMS, TEAM_STATES), 1.0, 6.0, ((0, 16),), jnp.float32),
    }


HIGHEST = lax.Precision.HIGHEST


def reference(transitions, states, cotangent, terminal, incidence, measured, obs_gain):
    incident = incidence.astype(jnp.float32)
    landmark = jnp.einsum('ktcr,ktrl->tcl', measured, incident, precision=HIGHEST)
    injection = jnp.einsum('tcl,ktrl->ktcr', landmark, incident, precision=HIGHEST)
    driven = cotangent + jnp.repeat(injection, STATES, axis=3) * obs_gain[:, None, None, :]

    def one_team(team_data):
        matrices, forward, forcing, final_cot = team_data

        def sweep_step(adjoint_next, pieces):
            matrix_now, state_now, force_now = pieces
            grad_now = jnp.einsum('cn,cm->nm', adjoint_next, state_now, precision=HIGHEST)
            adjoint_now = jnp.dot(adjoint_next, matrix_now, precision=HIGHEST) + force_now
            return adjoint_now, (adjoint_now, grad_now.astype(jnp.bfloat16))

        _, outputs = lax.scan(sweep_step, final_cot, (matrices, forward, forcing), reverse=True)
        return outputs

    adjoint, grad_transitions = lax.map(one_team, (transitions, states, driven, terminal))
    return adjoint, grad_transitions
```

```python
import jax
import jax.numpy as jnp
from jax import lax
from jax.sharding import PartitionSpec as P

STATES = 16
TEAM_STATES = 512
COLS = 64
ROBOTS = 32
LMK = 2048
TEAMS = 16
STEPS = 32
RING = 8
BOTH = ("team", "tm")

HIGH = lax.Precision.HIGH


def matmul(left, right):
    return jnp.dot(left, right, precision=HIGH)


def route(pairs_of):
    out = []
    for team in range(TEAMS):
        for ring in range(STEPS // RING):
            for src, dst in pairs_of(team % 2):
                base = team * STEPS + ring * RING
                out.append((base + src, base + dst))
    return out


def holder(pair, odd):
    return 2 * pair + odd


def partner(pair, odd):
    return 2 * pair + 1 - odd


def own_pair(odd):
    return 2 if odd else 1


def near_pair(odd):
    return 3 if odd else 0


def far_pair(odd):
    return 1 if odd else 2


def last_pair(odd):
    return 0 if odd else 3


TO_HOLDER = route(lambda odd: [(partner(p, odd), holder(p, odd)) for p in range(4)])
TO_PARTNER = [(dst, src) for src, dst in TO_HOLDER]


def between(source, target):
    return route(lambda odd: [(holder(source(odd), odd), holder(target(odd), odd))])


NEAR_IN = between(near_pair, own_pair)
FAR_IN = between(far_pair, own_pair)
LAST_STEP = between(last_pair, far_pair)
LAST_IN = between(last_pair, own_pair)
NEAR_OUT = between(own_pair, near_pair)
FAR_OUT = between(own_pair, far_pair)
LAST_OUT = between(own_pair, last_pair)


def ring_hop(ring):
    out = []
    for team in range(TEAMS):
        z = holder(own_pair(team % 2), team % 2)
        out.append((team * STEPS + ring * RING + z, team * STEPS + (ring - 1) * RING + z))
    return out


def send(value, pairs, name):
    with jax.named_scope(name):
        return lax.ppermute(value, BOTH, pairs)


def fold(rows):
    return jnp.concatenate([rows[..., :16, :], rows[..., 16:, :]], axis=-1)


def unfold(packed):
    return jnp.concatenate([packed[..., :64], packed[..., 64:]], axis=-2)


def shards(transitions, states, cotangent, terminal, incidence, measured, obs_gain):
    matrix = transitions[0, 0]
    state = states[0, 0]
    cot = cotangent[0, 0]
    team = lax.axis_index("team")
    step = lax.axis_index("tm")
    even = team % 2 == 0
    ring = step // RING

    def pick(a, b):
        return jnp.where(even, a, b)

    other_matrix = send(matrix, TO_HOLDER, "mpair")
    other_cot = send(cot, TO_HOLDER, "cpair")

    incident = incidence[0, 0].astype(jnp.float32)
    slices = incident.reshape(ROBOTS, TEAMS, LMK // TEAMS).transpose(1, 0, 2)
    packed = fold(measured[0, 0].T)
    packed = jnp.broadcast_to(packed[None], (TEAMS,) + packed.shape)
    with jax.named_scope("a2a_in"):
        got = lax.all_to_all(jnp.concatenate([slices, packed], axis=1), "team", 0, 0, tiled=True)
    rows = got[:, :ROBOTS].reshape(TEAMS * ROBOTS, LMK // TEAMS)
    seen = unfold(got[:, ROBOTS:]).reshape(TEAMS * ROBOTS, COLS)
    landmark = jnp.einsum("rc,rl->cl", seen, rows, precision=HIGH)
    part = jnp.einsum("rl,cl->rc", rows, landmark, precision=HIGH)
    part = fold(part.reshape(TEAMS, ROBOTS, COLS))
    with jax.named_scope("a2a_out"):
        parts = lax.all_to_all(part, "team", 0, 0, tiled=True)
    injected = jnp.sum(parts, axis=0)

    high = pick(other_matrix, matrix)
    low = pick(matrix, other_matrix)
    two = matmul(high, low)
    two_near = send(two, NEAR_IN, "pnear")
    two_far = send(two, FAR_IN, "pfar")
    two_passed = send(two, LAST_STEP, "plast1")
    two_last = send(two_passed, FAR_IN, "plast2")

    other_injected = send(injected, TO_HOLDER, "ipair")
    owner = jnp.arange(TEAM_STATES)[None, :] // STATES == jnp.arange(ROBOTS)[:, None]
    spread = jnp.where(owner, obs_gain[0][None, :], 0.0)

    def drive(direct, packed_rows):
        return direct + jnp.einsum("rc,rn->cn", unfold(packed_rows), spread, precision=HIGH)

    driven = drive(cot, injected)
    other_driven = drive(other_cot, other_injected)
    driven_high = pick(other_driven, driven)
    driven_low = pick(driven, other_driven)
    offset = matmul(driven_high, low) + driven_low
    off_near = send(offset, NEAR_IN, "dnear")
    off_far = send(offset, FAR_IN, "dfar")
    off_last = send(offset, LAST_IN, "dlast")

    maps = [pick(two_last, two_near), pick(two_far, two), pick(two, two_far), pick(two_near, two_last)]
    offs = [pick(off_last, off_near), pick(off_far, offset), pick(offset, off_far), pick(off_near, off_last)]
    eight = matmul(matmul(maps[0], maps[1]), matmul(maps[2], maps[3]))
    total = offs[0]
    for k in range(1, 4):
        total = matmul(total, maps[k]) + offs[k]

    incoming = terminal[0]
    for source in range(STEPS // RING - 1, 0, -1):
        leaving = matmul(incoming, eight) + total
        arrived = send(leaving, ring_hop(source), f"hop{source}")
        incoming = jnp.where(ring == source - 1, arrived, incoming)

    after = [incoming]
    for k in range(3):
        after.append(matmul(after[-1], maps[k]) + offs[k])
    to_near = send(pick(after[3], after[0]), NEAR_OUT, "bnear")
    to_far = send(pick(after[1], after[2]), FAR_OUT, "bfar")
    to_last = send(pick(after[0], after[3]), LAST_OUT, "blast")
    pair = (step % RING) // 2
    at_near = pair == pick(near_pair(0), near_pair(1))
    at_far = pair == pick(far_pair(0), far_pair(1))
    at_own = pair == pick(own_pair(0), own_pair(1))
    enter = jnp.where(at_own, pick(after[2], after[1]), jnp.where(at_near, to_near, jnp.where(at_far, to_far, to_last)))
    middle = matmul(enter, high) + driven_high
    passed = send(pick(enter, middle), TO_PARTNER, "bpair")
    holds = step % 2 == team % 2
    running = jnp.where(holds, pick(middle, enter), passed)
    grad = jnp.einsum("cn,cm->nm", running, state, precision=HIGH).astype(jnp.bfloat16)
    adjoint = matmul(running, matrix) + driven
    return adjoint[None, None], grad[None, None]


def solution(mesh):
    placed = (
        P("team", "tm", None, None),
        P("team", "tm", None, None),
        P("team", "tm", None, None),
        P("team", None, None),
        P("team", "tm", None, None),
        P("team", "tm", None, None),
        P("team", None),
    )
    return jax.shard_map(
        shards,
        mesh=mesh,
        in_specs=placed,
        out_specs=(P("team", "tm", None, None), P("team", "tm", None, None)),
        check_vma=False,
    )
```

```python
import jax
import jax.numpy as jnp
from jax import lax
from jax.sharding import PartitionSpec as P

STATES = 16
TEAM_STATES = 512
COLS = 64
ROBOTS = 32
LMK = 2048
TEAMS = 16
STEPS = 32
RING = 8
BOTH = ("team", "tm")

HIGH = lax.Precision.HIGH


def matmul(left, right):
    return jnp.dot(left, right, precision=HIGH)


def route(pairs_of):
    out = []
    for team in range(TEAMS):
        for ring in range(STEPS // RING):
            for src, dst in pairs_of(team % 2):
                base = team * STEPS + ring * RING
                out.append((base + src, base + dst))
    return out


def holder(pair, odd):
    return 2 * pair + odd


def partner(pair, odd):
    return 2 * pair + 1 - odd


def own_pair(odd):
    return 2 if odd else 1


def near_pair(odd):
    return 3 if odd else 0


def far_pair(odd):
    return 1 if odd else 2


def last_pair(odd):
    return 0 if odd else 3


TO_HOLDER = route(lambda odd: [(partner(p, odd), holder(p, odd)) for p in range(4)])
TO_PARTNER = [(dst, src) for src, dst in TO_HOLDER]


def between(source, target):
    return route(lambda odd: [(holder(source(odd), odd), holder(target(odd), odd))])


NEAR_IN = between(near_pair, own_pair)
FAR_IN = between(far_pair, own_pair)
LAST_STEP = between(last_pair, far_pair)
FIRST_IN = between(lambda odd: 0, own_pair)
FINAL_IN = between(lambda odd: 3, own_pair)
FIRST_OUT = between(own_pair, lambda odd: 0)
FINAL_OUT = between(own_pair, lambda odd: 3)
FAR_OUT = between(own_pair, far_pair)


def ring_hop(ring):
    out = []
    for team in range(TEAMS):
        z = holder(own_pair(team % 2), team % 2)
        out.append((team * STEPS + ring * RING + z, team * STEPS + (ring - 1) * RING + z))
    return out


def send(value, pairs):
    return lax.ppermute(value, BOTH, pairs)


def fold(rows):
    return jnp.concatenate([rows[..., :16, :], rows[..., 16:, :]], axis=-1)


def unfold(packed):
    return jnp.concatenate([packed[..., :64], packed[..., 64:]], axis=-2)


def shards(transitions, states, cotangent, terminal, incidence, measured, obs_gain):
    matrix = transitions[0, 0]
    state = states[0, 0]
    cot = cotangent[0, 0]
    team = lax.axis_index("team")
    step = lax.axis_index("tm")
    even = team % 2 == 0
    ring = step // RING

    def pick(a, b):
        return jnp.where(even, a, b)

    other_matrix = send(matrix, TO_HOLDER)
    other_cot = send(cot, TO_HOLDER)

    incident = incidence[0, 0].astype(jnp.float32)
    slices = incident.reshape(ROBOTS, TEAMS, LMK // TEAMS).transpose(1, 0, 2)
    packed = fold(measured[0, 0].T)
    packed = jnp.broadcast_to(packed[None], (TEAMS,) + packed.shape)
    got = lax.all_to_all(jnp.concatenate([slices, packed], axis=1), "team", 0, 0, tiled=True)
    rows = got[:, :ROBOTS].reshape(TEAMS * ROBOTS, LMK // TEAMS)
    seen = unfold(got[:, ROBOTS:]).reshape(TEAMS * ROBOTS, COLS)
    landmark = jnp.einsum("rc,rl->cl", seen, rows, precision=HIGH)
    part = jnp.einsum("rl,cl->rc", rows, landmark, precision=HIGH)
    part = fold(part.reshape(TEAMS, ROBOTS, COLS))
    parts = lax.all_to_all(part, "team", 0, 0, tiled=True)
    injected = jnp.sum(parts, axis=0)

    high = pick(other_matrix, matrix)
    low = pick(matrix, other_matrix)
    two = jnp.dot(high, low, precision=lax.Precision.HIGHEST)
    two_passed = send(two, LAST_STEP)
    two_near = send(two, NEAR_IN)
    two_far = send(two, FAR_IN)
    two_last = send(two_passed, FAR_IN)

    other_injected = send(injected, TO_HOLDER)
    owner = jnp.arange(TEAM_STATES)[None, :] // STATES == jnp.arange(ROBOTS)[:, None]
    spread = jnp.where(owner, obs_gain[0][None, :], 0.0)

    def drive(direct, packed_rows):
        return direct + jnp.einsum("rc,rn->cn", unfold(packed_rows), spread, precision=HIGH)

    driven = drive(cot, injected)
    other_driven = drive(other_cot, other_injected)
    driven_high = pick(other_driven, driven)
    driven_low = pick(driven, other_driven)
    offset = matmul(driven_high, low) + driven_low
    off0 = send(offset, FIRST_IN)
    off3 = send(offset, FINAL_IN)
    off_far = send(offset, FAR_IN)
    off1 = pick(offset, off_far)
    off2 = pick(off_far, offset)

    map3, map2, map1, map0 = pick(two_last, two_near), pick(two_far, two), pick(two, two_far), pick(two_near, two_last)
    enter1 = matmul(map3, map2)
    enter0 = matmul(enter1, map1)
    eight = matmul(enter0, map0)
    shift1 = matmul(off3, map2) + off2
    shift0 = matmul(shift1, map1) + off1
    total = matmul(shift0, map0) + off0
    enter_far, shift_far = pick(map3, enter1), pick(off3, shift1)
    enter_own, shift_own = pick(enter1, map3), pick(shift1, off3)

    incoming = terminal[0]
    before = jnp.where(ring == STEPS // RING - 1, incoming, 0.0)
    for source in range(STEPS // RING - 1, 0, -1):
        leaving = matmul(incoming, eight) + total
        incoming = send(leaving, ring_hop(source))
        if source > 1:
            before = jnp.where(ring == source - 1, incoming, before)
    incoming = jnp.where(ring == 0, incoming, before)

    to_final = send(incoming, FINAL_OUT)
    to_first = send(matmul(incoming, enter0) + shift0, FIRST_OUT)
    to_far = send(matmul(incoming, enter_far) + shift_far, FAR_OUT)
    at_own = matmul(incoming, enter_own) + shift_own
    pair = (step % RING) // 2
    is_own = pair == pick(own_pair(0), own_pair(1))
    enter = jnp.where(is_own, at_own, jnp.where(pair == 0, to_first, jnp.where(pair == 3, to_final, to_far)))
    middle = matmul(enter, high) + driven_high
    passed = send(pick(enter, middle), TO_PARTNER)
    holds = step % 2 == team % 2
    running = jnp.where(holds, pick(middle, enter), passed)
    grad = jnp.einsum("cn,cm->nm", running, state, precision=HIGH).astype(jnp.bfloat16)
    adjoint = matmul(running, matrix) + driven
    return adjoint[None, None], grad[None, None]


def solution(mesh):
    placed = (
        P("team", "tm", None, None),
        P("team", "tm", None, None),
        P("team", "tm", None, None),
        P("team", None, None),
        P("team", "tm", None, None),
        P("team", "tm", None, None),
        P("team", None),
    )
    return jax.shard_map(
        shards,
        mesh=mesh,
        in_specs=placed,
        out_specs=(P("team", "tm", None, None), P("team", "tm", None, None)),
        check_vma=False,
    )
```

```python
import jax
import jax.numpy as jnp
from jax import lax
from jax.sharding import PartitionSpec as P

STATES = 16
TEAM_STATES = 512
COLS = 64
ROBOTS = 32
LMK = 2048
TEAMS = 16
STEPS = 32
RING = 8
BOTH = ("team", "tm")

HIGH = lax.Precision.HIGH


def matmul(left, right):
    return jnp.dot(left, right, precision=HIGH)


def route(pairs_of):
    out = []
    for team in range(TEAMS):
        for ring in range(STEPS // RING):
            for src, dst in pairs_of(team % 2):
                base = team * STEPS + ring * RING
                out.append((base + src, base + dst))
    return out


def holder(pair, odd):
    return 2 * pair + odd


def partner(pair, odd):
    return 2 * pair + 1 - odd


def own_pair(odd):
    return 2 if odd else 1


def near_pair(odd):
    return 3 if odd else 0


def far_pair(odd):
    return 1 if odd else 2


def last_pair(odd):
    return 0 if odd else 3


TO_HOLDER = route(lambda odd: [(partner(p, odd), holder(p, odd)) for p in range(4)])
TO_PARTNER = [(dst, src) for src, dst in TO_HOLDER]


def between(source, target):
    return route(lambda odd: [(holder(source(odd), odd), holder(target(odd), odd))])


INWARD = route(
    lambda odd: [
        (holder(near_pair(odd), odd), holder(own_pair(odd), odd)),
        (holder(last_pair(odd), odd), holder(far_pair(odd), odd)),
    ]
)
FAR_IN = between(far_pair, own_pair)
FIRST_IN = between(lambda odd: 0, own_pair)
FINAL_IN = between(lambda odd: 3, own_pair)
FIRST_OUT = between(own_pair, lambda odd: 0)
FAR_OUT = between(own_pair, far_pair)


def down(target):
    out = []
    for team in range(TEAMS):
        odd = team % 2
        for ring in range(1, STEPS // RING):
            base = team * STEPS + ring * RING
            out.append((base + holder(own_pair(odd), odd), base - RING + holder(target(odd), odd)))
    return out


def ring_hop(ring):
    out = []
    for team in range(TEAMS):
        z = holder(own_pair(team % 2), team % 2)
        out.append((team * STEPS + ring * RING + z, team * STEPS + (ring - 1) * RING + z))
    return out


def send(value, pairs):
    return lax.ppermute(value, BOTH, pairs)


def fold(rows):
    return jnp.concatenate([rows[..., :16, :], rows[..., 16:, :]], axis=-1)


def unfold(packed):
    return jnp.concatenate([packed[..., :64], packed[..., 64:]], axis=-2)


def shards(transitions, states, cotangent, terminal, incidence, measured, obs_gain):
    matrix = transitions[0, 0]
    state = states[0, 0]
    cot = cotangent[0, 0]
    team = lax.axis_index("team")
    step = lax.axis_index("tm")
    even = team % 2 == 0
    ring = step // RING

    def pick(a, b):
        return jnp.where(even, a, b)

    other_matrix = send(matrix, TO_HOLDER)

    incident = incidence[0, 0].astype(jnp.float32)
    slices = incident.reshape(ROBOTS, TEAMS, LMK // TEAMS).transpose(1, 0, 2)
    packed = fold(measured[0, 0].T)
    packed = jnp.broadcast_to(packed[None], (TEAMS,) + packed.shape)
    got = lax.all_to_all(jnp.concatenate([slices, packed], axis=1), "team", 0, 0, tiled=True)
    rows = got[:, :ROBOTS].reshape(TEAMS * ROBOTS, LMK // TEAMS)
    seen = unfold(got[:, ROBOTS:]).reshape(TEAMS * ROBOTS, COLS)
    landmark = jnp.einsum("rc,rl->cl", seen, rows, precision=HIGH)
    part = jnp.einsum("rl,cl->rc", rows, landmark, precision=HIGH)
    part = fold(part.reshape(TEAMS, ROBOTS, COLS))
    parts = lax.all_to_all(part, "team", 0, 0, tiled=True)
    injected = jnp.sum(parts, axis=0)

    high = pick(other_matrix, matrix)
    low = pick(matrix, other_matrix)
    two = jnp.dot(high, low, precision=lax.Precision.HIGHEST)
    inward = send(two, INWARD)
    two_far = send(two, FAR_IN)
    two_last = send(inward, FAR_IN)

    owner = jnp.arange(TEAM_STATES)[None, :] // STATES == jnp.arange(ROBOTS)[:, None]
    spread = jnp.where(owner, obs_gain[0][None, :], 0.0)
    driven = cot + jnp.einsum("rc,rn->cn", unfold(injected), spread, precision=HIGH)
    other_driven = send(driven, TO_HOLDER)
    driven_high = pick(other_driven, driven)
    driven_low = pick(driven, other_driven)
    offset = matmul(driven_high, low) + driven_low
    off3 = send(offset, FINAL_IN)
    off_far = send(offset, FAR_IN)
    off0 = send(offset, FIRST_IN)

    map3, map2, map1, map0 = pick(two_last, inward), pick(two_far, two), pick(two, two_far), pick(inward, two_last)
    map3, map2, map1, map0 = lax.optimization_barrier((map3, map2, map1, map0))
    enter1 = matmul(map3, map2)
    enter0 = matmul(enter1, map1)
    eight = matmul(enter0, map0)
    enter_far = pick(map3, enter1)
    enter_own = pick(enter1, map3)
    eight, enter0, enter_far, enter_own, off3, off_far, off0 = lax.optimization_barrier(
        (eight, enter0, enter_far, enter_own, off3, off_far, off0)
    )
    off1 = pick(offset, off_far)
    off2 = pick(off_far, offset)
    shift1 = matmul(off3, map2) + off2
    shift0 = matmul(shift1, map1) + off1
    total = matmul(shift0, map0) + off0
    shift_far = pick(off3, shift1)
    shift_own = pick(shift1, off3)

    pair = (step % RING) // 2
    is_own = pair == pick(own_pair(0), own_pair(1))
    last_ring = STEPS // RING - 1
    leaving = matmul(terminal[0], eight) + total
    incoming = send(leaving, ring_hop(last_ring))
    map_first = send(enter0, FIRST_OUT)
    map_far = send(enter_far, FAR_OUT)
    shift_first = send(shift0, FIRST_OUT)
    shift_far = send(shift_far, FAR_OUT)
    out = leaving
    for source in range(last_ring - 1, 0, -1):
        leaving = matmul(incoming, eight) + total
        out = jnp.where(ring == source, leaving, out)
        if source > 1:
            incoming = send(leaving, ring_hop(source))
    parts = [
        send(out, down(lambda odd: 3)),
        send(out, down(lambda odd: 0)),
        send(out, down(far_pair)),
        send(out, down(own_pair)),
    ]
    enter_map = jnp.where(is_own, enter_own, jnp.where(pair == 0, map_first, map_far))
    enter_shift = jnp.where(is_own, shift_own, jnp.where(pair == 0, shift_first, shift_far))
    enter_map, enter_shift = lax.optimization_barrier((enter_map, enter_shift))
    entry = (parts[0] + parts[1]) + (parts[2] + parts[3]) + jnp.where(ring == last_ring, terminal[0], 0.0)
    entry = lax.optimization_barrier(entry)
    enter = jnp.where(pair == 3, entry, matmul(entry, enter_map) + enter_shift)
    enter = lax.optimization_barrier(enter)
    middle = matmul(enter, high) + driven_high
    passed = send(pick(enter, middle), TO_PARTNER)
    holds = step % 2 == team % 2
    running = jnp.where(holds, pick(middle, enter), passed)
    running = lax.optimization_barrier(running)
    grad = jnp.einsum("cn,cm->nm", running, state, precision=HIGH).astype(jnp.bfloat16)
    adjoint = matmul(running, matrix) + driven
    return adjoint[None, None], grad[None, None]


def solution(mesh):
    placed = (
        P("team", "tm", None, None),
        P("team", "tm", None, None),
        P("team", "tm", None, None),
        P("team", None, None),
        P("team", "tm", None, None),
        P("team", "tm", None, None),
        P("team", None),
    )
    return jax.shard_map(
        shards,
        mesh=mesh,
        in_specs=placed,
        out_specs=(P("team", "tm", None, None), P("team", "tm", None, None)),
        check_vma=False,
    )
```

```python
import jax
import jax.numpy as jnp
from jax import lax
from jax.experimental import pallas as pl
from jax.experimental.pallas import tpu as pltpu
from jax.sharding import PartitionSpec as P

STATES = 16
TEAM_STATES = 512
COLS = 64
ROBOTS = 32
LMK = 2048
TEAMS = 16
STEPS = 32
RING = 8
BOTH = ("team", "tm")

HIGH = lax.Precision.HIGH


def matmul(left, right):
    return jnp.dot(left, right, precision=HIGH)


def route(pairs_of):
    out = []
    for team in range(TEAMS):
        for ring in range(STEPS // RING):
            for src, dst in pairs_of(team % 2):
                base = team * STEPS + ring * RING
                out.append((base + src, base + dst))
    return out


def holder(pair, odd):
    return 2 * pair + odd


def partner(pair, odd):
    return 2 * pair + 1 - odd


NEAR = 0
FAR = 2


def own_pair(odd):
    return 3 if odd else 1


def last_pair(odd):
    return 1 if odd else 3


WORKER_PAIR = route(lambda odd: [(partner(own_pair(odd), odd), holder(own_pair(odd), odd))])
OTHER_PAIRS = route(
    lambda odd: [(partner(p, odd), holder(p, odd)) for p in range(4) if p != own_pair(odd)]
)
TO_HOLDER = route(lambda odd: [(partner(p, odd), holder(p, odd)) for p in range(4)])
TO_PARTNER = [(dst, src) for src, dst in TO_HOLDER]


def between(source, target, only_odd=False):
    def pairs_of(odd):
        if only_odd and not odd:
            return []
        return [(holder(source(odd), odd), holder(target(odd), odd))]

    return route(pairs_of)


def near_pair(odd):
    return NEAR


def far_pair(odd):
    return FAR


LAST_STEP = between(last_pair, far_pair)
FAR_IN = between(far_pair, own_pair)
NEAR_IN = between(near_pair, own_pair)
LAST_IN = between(last_pair, own_pair)
NEAR_OUT = between(own_pair, near_pair)
FAR_OUT = between(own_pair, far_pair)
FAR_OUT_ODD = between(own_pair, far_pair, True)
LAST_OUT_ODD = between(own_pair, last_pair, True)


def down(target):
    out = []
    for team in range(TEAMS):
        odd = team % 2
        for ring in range(1, STEPS // RING):
            base = team * STEPS + ring * RING
            out.append((base + holder(own_pair(odd), odd), base - RING + holder(target(odd), odd)))
    return out


def ring_hop(ring):
    out = []
    for team in range(TEAMS):
        z = holder(own_pair(team % 2), team % 2)
        out.append((team * STEPS + ring * RING + z, team * STEPS + (ring - 1) * RING + z))
    return out


def send(value, pairs):
    return lax.ppermute(value, BOTH, pairs)


def fold(rows):
    return jnp.concatenate([rows[..., :16, :], rows[..., 16:, :]], axis=-1)


def unfold(packed):
    return jnp.concatenate([packed[..., :64], packed[..., 64:]], axis=-2)


def split(value):
    high = value.astype(jnp.bfloat16)
    return high, (value - high.astype(jnp.float32)).astype(jnp.bfloat16)


def product(left, right, dims=(((1,), (0,)), ((), ()))):
    def one(a, b):
        return lax.dot_general(a, b, dims, preferred_element_type=jnp.float32)

    return one(left[0], right[0]) + (one(left[0], right[1]) + one(left[1], right[0]))


def compose_kernel(flag, two, last, far, near, enter1, enter0, eight, m3, m2, m1, m0, r1, r0, r8, sems, out_sems):
    def load(src, dst, k):
        return pltpu.make_async_copy(src, dst, sems.at[k])

    def store(src, dst, k):
        return pltpu.make_async_copy(src, dst, out_sems.at[k])

    @pl.when(flag[0] == 1)
    def _():
        load(last, m3, 0).start()
        load(two, m1, 2).start()

    @pl.when(flag[0] == 0)
    def _():
        load(two, m3, 0).start()
        load(last, m1, 2).start()

    load(far, m2, 1).start()
    load(near, m0, 3).start()
    load(last, m3, 0).wait()
    load(far, m2, 1).wait()
    r1[...] = product(split(m3[...]), split(m2[...]))
    store(r1, enter1, 0).start()
    load(last, m1, 2).wait()
    r0[...] = product(split(r1[...]), split(m1[...]))
    store(r0, enter0, 1).start()
    load(near, m0, 3).wait()
    r8[...] = product(split(r0[...]), split(m0[...]))
    store(r8, eight, 2).start()
    store(r1, enter1, 0).wait()
    store(r0, enter0, 1).wait()
    store(r8, eight, 2).wait()


def compose(even, two, last, far, near):
    shape = (TEAM_STATES, TEAM_STATES)
    return pl.pallas_call(
        compose_kernel,
        out_shape=[jax.ShapeDtypeStruct(shape, jnp.float32)] * 3,
        in_specs=[pl.BlockSpec(memory_space=pltpu.SMEM)] + [pl.BlockSpec(memory_space=pl.ANY)] * 4,
        out_specs=[pl.BlockSpec(memory_space=pl.ANY)] * 3,
        scratch_shapes=[pltpu.VMEM(shape, jnp.float32)] * 7
        + [pltpu.SemaphoreType.DMA((4,)), pltpu.SemaphoreType.DMA((3,))],
        name="compose",
    )(even.astype(jnp.int32)[None], two, last, far, near)


def landmark_kernel(got, part):
    rows = got[:, :ROBOTS, :].reshape(TEAMS * ROBOTS, LMK // TEAMS).astype(jnp.bfloat16)
    packed = got[:, ROBOTS:, :]
    seen = jnp.concatenate([packed[..., :COLS], packed[..., COLS:]], axis=1).reshape(TEAMS * ROBOTS, COLS)

    def one(a, b, left, right):
        return lax.dot_general(a, b, (((left,), (right,)), ((), ())), preferred_element_type=jnp.float32)

    first, second = split(seen)
    landmark = one(first, rows, 0, 0) + one(second, rows, 0, 0)
    first, second = split(landmark)
    back = (one(rows, first, 1, 1) + one(rows, second, 1, 1)).reshape(TEAMS, ROBOTS, COLS)
    part[..., :COLS] = back[:, : ROBOTS // 2, :]
    part[..., COLS:] = back[:, ROBOTS // 2 :, :]


def shards(transitions, states, cotangent, terminal, incidence, measured, obs_gain):
    matrix = transitions[0, 0]
    state = states[0, 0]
    cot = cotangent[0, 0]
    team = lax.axis_index("team")
    step = lax.axis_index("tm")
    even = team % 2 == 0
    ring = step // RING

    def pick(a, b):
        return jnp.where(even, a, b)

    other_matrix = send(matrix, TO_HOLDER)

    incident = incidence[0, 0].astype(jnp.float32)
    slices = incident.reshape(ROBOTS, TEAMS, LMK // TEAMS).transpose(1, 0, 2)
    packed = fold(measured[0, 0].T)
    packed = jnp.broadcast_to(packed[None], (TEAMS,) + packed.shape)
    got = lax.all_to_all(jnp.concatenate([slices, packed], axis=1), "team", 0, 0, tiled=True)
    part = pl.pallas_call(
        landmark_kernel,
        out_shape=jax.ShapeDtypeStruct((TEAMS, ROBOTS // 2, 2 * COLS), jnp.float32),
        name="landmark",
    )(got)
    parts = lax.all_to_all(part, "team", 0, 0, tiled=True)
    injected = jnp.sum(parts, axis=0)

    high = pick(other_matrix, matrix)
    low = pick(matrix, other_matrix)
    two = jnp.dot(high, low, precision=lax.Precision.HIGHEST)
    passing = send(two, LAST_STEP)
    two_far = send(two, FAR_IN)
    two_near = send(two, NEAR_IN)
    two_last = send(passing, FAR_IN)

    owner = jnp.arange(TEAM_STATES)[None, :] // STATES == jnp.arange(ROBOTS)[:, None]
    spread = jnp.where(owner, obs_gain[0][None, :], 0.0)
    driven = cot + jnp.einsum("rc,rn->cn", unfold(injected), spread, precision=HIGH)
    other_driven = send(driven, OTHER_PAIRS)
    own_driven = send(driven, WORKER_PAIR)

    def compose_driven(other):
        later, sooner = pick(other, driven), pick(driven, other)
        return later, matmul(later, low) + sooner

    later, offset = compose_driven(other_driven)
    off_last = send(offset, LAST_IN)
    off_far = send(offset, FAR_IN)
    off_near = send(offset, NEAR_IN)

    map1 = pick(two, two_last)
    enter1, enter0, eight = compose(even, two, two_last, two_far, two_near)
    eight, enter0, enter1, off_last, off_far, off_near = lax.optimization_barrier(
        (eight, enter0, enter1, off_last, off_far, off_near)
    )
    own_later, own_offset = compose_driven(own_driven)
    off3 = pick(off_last, own_offset)
    off1 = pick(own_offset, off_last)
    shift1 = matmul(off3, two_far) + off_far
    shift0 = matmul(shift1, map1) + off1
    total = matmul(shift0, two_near) + off_near

    last_ring = STEPS // RING - 1
    leaving = matmul(terminal[0], eight) + total
    incoming = send(leaving, ring_hop(last_ring))
    map_near = send(enter0, NEAR_OUT)
    map_far = send(two, FAR_OUT_ODD)
    map_last = send(enter1, LAST_OUT_ODD)
    shift_near = send(shift0, NEAR_OUT)
    shift_far = send(off3, FAR_OUT)
    shift_last = send(shift1, LAST_OUT_ODD)
    out = leaving
    for source in range(last_ring - 1, 0, -1):
        leaving = matmul(incoming, eight) + total
        out = jnp.where(ring == source, leaving, out)
        if source > 1:
            incoming = send(leaving, ring_hop(source))
    arrived = [
        send(out, down(last_pair)), send(out, down(near_pair)), send(out, down(far_pair)), send(out, down(own_pair))
    ]
    pair = (step % RING) // 2
    enter_map = jnp.where(pair == NEAR, map_near, jnp.where(pair == FAR, pick(passing, map_far), pick(enter1, map_last)))
    enter_shift = jnp.where(pair == NEAR, shift_near, jnp.where(pair == FAR, shift_far, pick(shift1, shift_last)))
    enter_map, enter_shift = lax.optimization_barrier((enter_map, enter_shift))
    entry = (arrived[0] + arrived[1]) + (arrived[2] + arrived[3]) + jnp.where(ring == last_ring, terminal[0], 0.0)
    entry = lax.optimization_barrier(entry)
    enter = jnp.where(pair == 3, entry, matmul(entry, enter_map) + enter_shift)
    enter = lax.optimization_barrier(enter)
    driven_high = jnp.where(pair == pick(own_pair(0), own_pair(1)), own_later, later)
    middle = matmul(enter, high) + driven_high
    passed = send(pick(enter, middle), TO_PARTNER)
    holds = step % 2 == team % 2
    running = jnp.where(holds, pick(middle, enter), passed)
    running = lax.optimization_barrier(running)
    grad = jnp.einsum("cn,cm->nm", running, state, precision=HIGH).astype(jnp.bfloat16)
    adjoint = matmul(running, matrix) + driven
    return adjoint[None, None], grad[None, None]


def solution(mesh):
    placed = (
        P("team", "tm", None, None),
        P("team", "tm", None, None),
        P("team", "tm", None, None),
        P("team", None, None),
        P("team", "tm", None, None),
        P("team", "tm", None, None),
        P("team", None),
    )
    return jax.shard_map(
        shards,
        mesh=mesh,
        in_specs=placed,
        out_specs=(P("team", "tm", None, None), P("team", "tm", None, None)),
        check_vma=False,
    )
```

```python
import jax
import jax.numpy as jnp
from jax import lax
from jax.experimental import pallas as pl
from jax.experimental.pallas import tpu as pltpu
from jax.sharding import PartitionSpec as P

STATES = 16
TEAM_STATES = 512
COLS = 64
ROBOTS = 32
LMK = 2048
TEAMS = 16
STEPS = 32
RING = 8
BOTH = ("team", "tm")

HIGH = lax.Precision.HIGH


def matmul(left, right):
    return jnp.dot(left, right, precision=HIGH)


def route(pairs_of):
    out = []
    for team in range(TEAMS):
        for ring in range(STEPS // RING):
            for src, dst in pairs_of(team % 2):
                base = team * STEPS + ring * RING
                out.append((base + src, base + dst))
    return out


def holder(pair, odd):
    return 2 * pair + odd


def partner(pair, odd):
    return 2 * pair + 1 - odd


NEAR = 0
FAR = 2


def own_pair(odd):
    return 3 if odd else 1


def last_pair(odd):
    return 1 if odd else 3


WORKER_PAIR = route(lambda odd: [(partner(own_pair(odd), odd), holder(own_pair(odd), odd))])
OTHER_PAIRS = route(
    lambda odd: [(partner(p, odd), holder(p, odd)) for p in range(4) if p != own_pair(odd)]
)
TO_HOLDER = route(lambda odd: [(partner(p, odd), holder(p, odd)) for p in range(4)])
TO_PARTNER = [(dst, src) for src, dst in TO_HOLDER]


def between(source, target, only_odd=False):
    def pairs_of(odd):
        if only_odd and not odd:
            return []
        return [(holder(source(odd), odd), holder(target(odd), odd))]

    return route(pairs_of)


def near_pair(odd):
    return NEAR


def far_pair(odd):
    return FAR


LAST_STEP = between(last_pair, far_pair)
FAR_IN = between(far_pair, own_pair)
NEAR_IN = between(near_pair, own_pair)
LAST_IN = between(last_pair, own_pair)
NEAR_OUT = between(own_pair, near_pair)
FAR_OUT = between(own_pair, far_pair)
FAR_OUT_ODD = between(own_pair, far_pair, True)
LAST_OUT_ODD = between(own_pair, last_pair, True)


def down(target):
    out = []
    for team in range(TEAMS):
        odd = team % 2
        for ring in range(1, STEPS // RING):
            base = team * STEPS + ring * RING
            out.append((base + holder(own_pair(odd), odd), base - RING + holder(target(odd), odd)))
    return out


def ring_hop(ring):
    out = []
    for team in range(TEAMS):
        z = holder(own_pair(team % 2), team % 2)
        out.append((team * STEPS + ring * RING + z, team * STEPS + (ring - 1) * RING + z))
    return out


def send(value, pairs):
    return lax.ppermute(value, BOTH, pairs)


def fold(rows):
    return jnp.concatenate([rows[..., :16, :], rows[..., 16:, :]], axis=-1)


def unfold(packed):
    return jnp.concatenate([packed[..., :64], packed[..., 64:]], axis=-2)


def split(value):
    high = value.astype(jnp.bfloat16)
    return high, (value - high.astype(jnp.float32)).astype(jnp.bfloat16)


def product(left, right, dims=(((1,), (0,)), ((), ()))):
    def one(a, b):
        return lax.dot_general(a, b, dims, preferred_element_type=jnp.float32)

    return one(left[0], right[0]) + (one(left[0], right[1]) + one(left[1], right[0]))


def copier(sems):
    return lambda src, dst, k: pltpu.make_async_copy(src, dst, sems.at[k])


def compose_kernel(flag, two, last, far, near, enter1, enter0, eight, m3, m2, m1, m0, r1, r0, r8, sems, out_sems):
    load, store = copier(sems), copier(out_sems)
    even = flag[0] == 1

    @pl.when(even)
    def _():
        load(last, m3, 0).start()
        load(two, m1, 2).start()

    @pl.when(jnp.logical_not(even))
    def _():
        load(two, m3, 0).start()
        load(last, m1, 2).start()

    load(far, m2, 1).start()
    load(near, m0, 3).start()
    load(last, m3, 0).wait()
    load(far, m2, 1).wait()
    r1[...] = product(split(m3[...]), split(m2[...]))
    store(r1, enter1, 0).start()
    load(last, m1, 2).wait()
    r0[...] = product(split(r1[...]), split(m1[...]))
    store(r0, enter0, 1).start()
    load(near, m0, 3).wait()
    r8[...] = product(split(r0[...]), split(m0[...]))
    store(r8, eight, 2).start()
    store(r1, enter1, 0).wait()
    store(r0, enter0, 1).wait()
    store(r8, eight, 2).wait()


SQUARE = (TEAM_STATES, TEAM_STATES)
ROWS = (COLS, TEAM_STATES)


def compose(flag, two, last, far, near):
    return pl.pallas_call(
        compose_kernel,
        out_shape=[jax.ShapeDtypeStruct(SQUARE, jnp.float32)] * 3,
        in_specs=[pl.BlockSpec(memory_space=pltpu.SMEM)] + [pl.BlockSpec(memory_space=pl.ANY)] * 4,
        out_specs=[pl.BlockSpec(memory_space=pl.ANY)] * 3,
        scratch_shapes=[pltpu.VMEM(SQUARE, jnp.float32)] * 7
        + [pltpu.SemaphoreType.DMA((4,)), pltpu.SemaphoreType.DMA((3,))],
        name="compose",
    )(flag, two, last, far, near)


def shift_kernel(
    flag, two, last, far, near, eight, off_own, off_last, off_far, off_near, start,
    shift2, shift1, shift0, total, leaving, m2, m1, m0, m8, sems,
):
    load = copier(sems)
    even = flag[0] == 1
    load(far, m2, 0).start()

    @pl.when(even)
    def _():
        load(two, m1, 1).start()

    @pl.when(jnp.logical_not(even))
    def _():
        load(last, m1, 1).start()

    load(near, m0, 2).start()
    load(eight, m8, 3).start()
    moved = jnp.where(even, off_last[...], off_own[...])
    off1 = jnp.where(even, off_own[...], off_last[...])
    shift2[...] = moved
    load(far, m2, 0).wait()
    moved = product(split(moved), split(m2[...])) + off_far[...]
    shift1[...] = moved
    load(last, m1, 1).wait()
    moved = product(split(moved), split(m1[...])) + off1
    shift0[...] = moved
    load(near, m0, 2).wait()
    moved = product(split(moved), split(m0[...])) + off_near[...]
    total[...] = moved
    load(eight, m8, 3).wait()
    leaving[...] = product(split(start[...]), split(m8[...])) + moved


def shift(flag, maps, rows):
    return pl.pallas_call(
        shift_kernel,
        out_shape=[jax.ShapeDtypeStruct(ROWS, jnp.float32)] * 5,
        in_specs=[pl.BlockSpec(memory_space=pltpu.SMEM)]
        + [pl.BlockSpec(memory_space=pl.ANY)] * 5
        + [pl.BlockSpec(memory_space=pltpu.VMEM)] * 5,
        out_specs=[pl.BlockSpec(memory_space=pltpu.VMEM)] * 5,
        scratch_shapes=[pltpu.VMEM(SQUARE, jnp.float32)] * 4 + [pltpu.SemaphoreType.DMA((4,))],
        name="shift",
    )(flag, *maps, *rows)


def hop_kernel(flag, arrived, eight, total, kept, out):
    @pl.when(flag[0] == 1)
    def _():
        out[...] = product(split(arrived[...]), split(eight[...])) + total[...]

    @pl.when(flag[0] == 0)
    def _():
        out[...] = kept[...]


def hop(flag, arrived, eight, total, kept):
    return pl.pallas_call(
        hop_kernel,
        out_shape=jax.ShapeDtypeStruct(ROWS, jnp.float32),
        in_specs=[pl.BlockSpec(memory_space=pltpu.SMEM)] + [pl.BlockSpec(memory_space=pltpu.VMEM)] * 4,
        out_specs=pl.BlockSpec(memory_space=pltpu.VMEM),
        name="hop",
    )(flag, arrived, eight, total, kept)


def landmark_kernel(got, part):
    rows = got[:, :ROBOTS, :].reshape(TEAMS * ROBOTS, LMK // TEAMS).astype(jnp.bfloat16)
    packed = got[:, ROBOTS:, :]
    seen = jnp.concatenate([packed[..., :COLS], packed[..., COLS:]], axis=1).reshape(TEAMS * ROBOTS, COLS)

    def one(a, b, left, right):
        return lax.dot_general(a, b, (((left,), (right,)), ((), ())), preferred_element_type=jnp.float32)

    first, second = split(seen)
    landmark = one(first, rows, 0, 0) + one(second, rows, 0, 0)
    first, second = split(landmark)
    back = (one(rows, first, 1, 1) + one(rows, second, 1, 1)).reshape(TEAMS, ROBOTS, COLS)
    part[..., :COLS] = back[:, : ROBOTS // 2, :]
    part[..., COLS:] = back[:, ROBOTS // 2 :, :]


def shards(transitions, states, cotangent, terminal, incidence, measured, obs_gain):
    matrix = transitions[0, 0]
    state = states[0, 0]
    cot = cotangent[0, 0]
    team = lax.axis_index("team")
    step = lax.axis_index("tm")
    even = team % 2 == 0
    ring = step // RING

    def pick(a, b):
        return jnp.where(even, a, b)

    other_matrix = send(matrix, TO_HOLDER)

    incident = incidence[0, 0].astype(jnp.float32)
    slices = incident.reshape(ROBOTS, TEAMS, LMK // TEAMS).transpose(1, 0, 2)
    packed = fold(measured[0, 0].T)
    packed = jnp.broadcast_to(packed[None], (TEAMS,) + packed.shape)
    got = lax.all_to_all(jnp.concatenate([slices, packed], axis=1), "team", 0, 0, tiled=True)
    part = pl.pallas_call(
        landmark_kernel,
        out_shape=jax.ShapeDtypeStruct((TEAMS, ROBOTS // 2, 2 * COLS), jnp.float32),
        name="landmark",
    )(got)
    parts = lax.all_to_all(part, "team", 0, 0, tiled=True)
    injected = jnp.sum(parts, axis=0)

    high = pick(other_matrix, matrix)
    low = pick(matrix, other_matrix)
    two = jnp.dot(high, low, precision=lax.Precision.HIGHEST)
    passing = send(two, LAST_STEP)
    two_far = send(two, FAR_IN)
    two_near = send(two, NEAR_IN)
    two_last = send(passing, FAR_IN)

    owner = jnp.arange(TEAM_STATES)[None, :] // STATES == jnp.arange(ROBOTS)[:, None]
    spread = lax.optimization_barrier(jnp.where(owner, obs_gain[0][None, :], 0.0))
    driven = cot + jnp.einsum("rc,rn->cn", unfold(injected), spread, precision=HIGH)
    other_driven = send(driven, OTHER_PAIRS)
    own_driven = send(driven, WORKER_PAIR)

    def compose_driven(other):
        later, sooner = pick(other, driven), pick(driven, other)
        return later, matmul(later, low) + sooner

    later, offset = compose_driven(other_driven)
    off_last = send(offset, LAST_IN)
    off_far = send(offset, FAR_IN)
    off_near = send(offset, NEAR_IN)

    own_later, own_offset = lax.optimization_barrier(compose_driven(own_driven))
    flag = even.astype(jnp.int32)[None]
    enter1, enter0, eight = compose(flag, two, two_last, two_far, two_near)
    off3, shift1, shift0, total, leaving = shift(
        flag,
        (two, two_last, two_far, two_near, eight),
        (own_offset, off_last, off_far, off_near, terminal[0]),
    )

    last_ring = STEPS // RING - 1
    incoming = send(leaving, ring_hop(last_ring))
    map_near = send(enter0, NEAR_OUT)
    map_far = send(two, FAR_OUT_ODD)
    map_last = send(enter1, LAST_OUT_ODD)
    shift_near = send(shift0, NEAR_OUT)
    shift_far = send(off3, FAR_OUT)
    shift_last = send(shift1, LAST_OUT_ODD)
    out = leaving
    for source in range(last_ring - 1, 0, -1):
        out = hop((ring == source).astype(jnp.int32)[None], incoming, eight, total, out)
        if source > 1:
            incoming = send(out, ring_hop(source))
    arrived = [
        send(out, down(last_pair)),
        send(out, down(near_pair)),
        send(out, down(far_pair)),
        send(out, down(own_pair)),
    ]
    pair = (step % RING) // 2
    enter_map = jnp.where(pair == NEAR, map_near, jnp.where(pair == FAR, pick(passing, map_far), pick(enter1, map_last)))
    enter_shift = jnp.where(pair == NEAR, shift_near, jnp.where(pair == FAR, shift_far, pick(shift1, shift_last)))
    enter_map, enter_shift = lax.optimization_barrier((enter_map, enter_shift))
    entry = (arrived[0] + arrived[1]) + (arrived[2] + arrived[3]) + jnp.where(ring == last_ring, terminal[0], 0.0)
    entry = lax.optimization_barrier(entry)
    enter = jnp.where(pair == 3, entry, matmul(entry, enter_map) + enter_shift)
    enter = lax.optimization_barrier(enter)
    driven_high = jnp.where(pair == pick(own_pair(0), own_pair(1)), own_later, later)
    middle = matmul(enter, high) + driven_high
    passed = send(pick(enter, middle), TO_PARTNER)
    holds = step % 2 == team % 2
    running = jnp.where(holds, pick(middle, enter), passed)
    running = lax.optimization_barrier(running)
    grad = jnp.einsum("cn,cm->nm", running, state, precision=HIGH).astype(jnp.bfloat16)
    adjoint = matmul(running, matrix) + driven
    return adjoint[None, None], grad[None, None]


def solution(mesh):
    placed = (
        P("team", "tm", None, None),
        P("team", "tm", None, None),
        P("team", "tm", None, None),
        P("team", None, None),
        P("team", "tm", None, None),
        P("team", "tm", None, None),
        P("team", None),
    )
    return jax.shard_map(
        shards,
        mesh=mesh,
        in_specs=placed,
        out_specs=(P("team", "tm", None, None), P("team", "tm", None, None)),
        check_vma=False,
    )
```

```python
import jax
import jax.numpy as jnp
from jax import lax
from jax.experimental import pallas as pl
from jax.experimental.pallas import tpu as pltpu
from jax.sharding import PartitionSpec as P

STATES = 16
TEAM_STATES = 512
COLS = 64
ROBOTS = 32
LMK = 2048
TEAMS = 16
STEPS = 32
RING = 8
BOTH = ("team", "tm")

HIGH = lax.Precision.HIGH


def matmul(left, right):
    return jnp.dot(left, right, precision=HIGH)


def route(pairs_of):
    out = []
    for team in range(TEAMS):
        for ring in range(STEPS // RING):
            for src, dst in pairs_of(team % 2):
                base = team * STEPS + ring * RING
                out.append((base + src, base + dst))
    return out


def holder(pair, odd):
    return 2 * pair + odd


def partner(pair, odd):
    return 2 * pair + 1 - odd


NEAR = 0
FAR = 2


def own_pair(odd):
    return 3 if odd else 1


def last_pair(odd):
    return 1 if odd else 3


WORKER_PAIR = route(lambda odd: [(partner(own_pair(odd), odd), holder(own_pair(odd), odd))])
OTHER_PAIRS = route(
    lambda odd: [(partner(p, odd), holder(p, odd)) for p in range(4) if p != own_pair(odd)]
)
TO_HOLDER = route(lambda odd: [(partner(p, odd), holder(p, odd)) for p in range(4)])
TO_PARTNER = [(dst, src) for src, dst in TO_HOLDER]


def between(source, target, only_odd=False):
    def pairs_of(odd):
        if only_odd and not odd:
            return []
        return [(holder(source(odd), odd), holder(target(odd), odd))]

    return route(pairs_of)


def near_pair(odd):
    return NEAR


def far_pair(odd):
    return FAR


LAST_STEP = between(last_pair, far_pair)
FAR_IN = between(far_pair, own_pair)
NEAR_IN = between(near_pair, own_pair)
LAST_IN = between(last_pair, own_pair)
NEAR_OUT = between(own_pair, near_pair)
FAR_OUT = between(own_pair, far_pair)
FAR_OUT_ODD = between(own_pair, far_pair, True)
LAST_OUT_ODD = between(own_pair, last_pair, True)


def down(target):
    out = []
    for team in range(TEAMS):
        odd = team % 2
        for ring in range(1, STEPS // RING):
            base = team * STEPS + ring * RING
            out.append((base + holder(own_pair(odd), odd), base - RING + holder(target(odd), odd)))
    return out


def ring_hop(ring):
    out = []
    for team in range(TEAMS):
        z = holder(own_pair(team % 2), team % 2)
        out.append((team * STEPS + ring * RING + z, team * STEPS + (ring - 1) * RING + z))
    return out


def send(value, pairs):
    return lax.ppermute(value, BOTH, pairs)


def fold(rows):
    return jnp.concatenate([rows[..., :16, :], rows[..., 16:, :]], axis=-1)


def unfold(packed):
    return jnp.concatenate([packed[..., :64], packed[..., 64:]], axis=-2)


def split(value):
    high = value.astype(jnp.bfloat16)
    return high, (value - high.astype(jnp.float32)).astype(jnp.bfloat16)


def product(left, right, dims=(((1,), (0,)), ((), ()))):
    def one(a, b):
        return lax.dot_general(a, b, dims, preferred_element_type=jnp.float32)

    return one(left[0], right[0]) + (one(left[0], right[1]) + one(left[1], right[0]))


def copier(sems):
    return lambda src, dst, k: pltpu.make_async_copy(src, dst, sems.at[k])


def compose_kernel(
    flag, two, last, far, near, shift1, shift0, enter1, enter0, eight, m3, m2, m1, m0, r1, r0, r8, sems, out_sems
):
    load, store = copier(sems), copier(out_sems)
    even = flag[0] == 1

    @pl.when(even)
    def _():
        load(last, m3, 0).start()
        load(two, m1, 2).start()

    @pl.when(jnp.logical_not(even))
    def _():
        load(two, m3, 0).start()
        load(last, m1, 2).start()

    load(far, m2, 1).start()
    load(near, m0, 3).start()
    map_rows, shift_rows = pl.ds(0, TEAM_STATES), pl.ds(TEAM_STATES, COLS)
    store(shift1, enter1.at[shift_rows], 3).start()
    store(shift0, enter0.at[shift_rows], 4).start()
    load(last, m3, 0).wait()
    load(far, m2, 1).wait()
    r1[...] = product(split(m3[...]), split(m2[...]))
    store(r1, enter1.at[map_rows], 0).start()
    load(last, m1, 2).wait()
    r0[...] = product(split(r1[...]), split(m1[...]))
    store(r0, enter0.at[map_rows], 1).start()
    load(near, m0, 3).wait()
    r8[...] = product(split(r0[...]), split(m0[...]))
    store(r8, eight, 2).start()
    store(shift1, enter1.at[shift_rows], 3).wait()
    store(shift0, enter0.at[shift_rows], 4).wait()
    store(r1, enter1.at[map_rows], 0).wait()
    store(r0, enter0.at[map_rows], 1).wait()
    store(r8, eight, 2).wait()


SQUARE = (TEAM_STATES, TEAM_STATES)
ROWS = (COLS, TEAM_STATES)
TALL = (TEAM_STATES + COLS, TEAM_STATES)


def compose(flag, maps, shifts):
    return pl.pallas_call(
        compose_kernel,
        out_shape=[jax.ShapeDtypeStruct(shape, jnp.float32) for shape in (TALL, TALL, SQUARE)],
        in_specs=[pl.BlockSpec(memory_space=pltpu.SMEM)] + [pl.BlockSpec(memory_space=pl.ANY)] * 6,
        out_specs=[pl.BlockSpec(memory_space=pl.ANY)] * 3,
        scratch_shapes=[pltpu.VMEM(SQUARE, jnp.float32)] * 7
        + [pltpu.SemaphoreType.DMA((4,)), pltpu.SemaphoreType.DMA((5,))],
        name="compose",
    )(flag, *maps, *shifts)


def sweep_kernel(
    flag, two, last, far, near, off_own, off_last, off_far, off_near, start,
    shift2, shift1, shift0, total, leaving, m3, m2, m1, m0, sems,
):
    load = copier(sems)
    even = flag[0] == 1

    @pl.when(even)
    def _():
        load(last, m3, 0).start()
        load(far, m2, 1).start()
        load(two, m1, 2).start()

    @pl.when(jnp.logical_not(even))
    def _():
        load(two, m3, 0).start()
        load(far, m2, 1).start()
        load(last, m1, 2).start()

    load(near, m0, 3).start()
    off3 = jnp.where(even, off_last[...], off_own[...])
    off1 = jnp.where(even, off_own[...], off_last[...])
    shift2[...] = off3
    load(last, m3, 0).wait()
    moved = product(split(start[...]), split(m3[...])) + off3
    both = jnp.concatenate([moved, off3], axis=0)

    def step(rows, weight, offset):
        return product(split(rows), split(weight)) + jnp.concatenate([offset, offset], axis=0)

    load(far, m2, 1).wait()
    both = step(both, m2[...], off_far[...])
    shift1[...] = both[COLS:]
    load(last, m1, 2).wait()
    both = step(both, m1[...], off1)
    shift0[...] = both[COLS:]
    load(near, m0, 3).wait()
    both = step(both, m0[...], off_near[...])
    total[...] = both[COLS:]
    leaving[...] = both[:COLS]


def sweep(flag, maps, rows):
    return pl.pallas_call(
        sweep_kernel,
        out_shape=[jax.ShapeDtypeStruct(ROWS, jnp.float32)] * 5,
        in_specs=[pl.BlockSpec(memory_space=pltpu.SMEM)]
        + [pl.BlockSpec(memory_space=pl.ANY)] * 4
        + [pl.BlockSpec(memory_space=pltpu.VMEM)] * 5,
        out_specs=[pl.BlockSpec(memory_space=pltpu.VMEM)] * 5,
        scratch_shapes=[pltpu.VMEM(SQUARE, jnp.float32)] * 4 + [pltpu.SemaphoreType.DMA((4,))],
        name="sweep",
    )(flag, *maps, *rows)


def hop_kernel(flag, arrived, eight, total, kept, out):
    @pl.when(flag[0] == 1)
    def _():
        out[...] = product(split(arrived[...]), split(eight[...])) + total[...]

    @pl.when(flag[0] == 0)
    def _():
        out[...] = kept[...]


def hop(flag, arrived, eight, total, kept):
    return pl.pallas_call(
        hop_kernel,
        out_shape=jax.ShapeDtypeStruct(ROWS, jnp.float32),
        in_specs=[pl.BlockSpec(memory_space=pltpu.SMEM)] + [pl.BlockSpec(memory_space=pltpu.VMEM)] * 4,
        out_specs=pl.BlockSpec(memory_space=pltpu.VMEM),
        name="hop",
    )(flag, arrived, eight, total, kept)


def landmark_kernel(got, part):
    rows = got[:, :ROBOTS, :].reshape(TEAMS * ROBOTS, LMK // TEAMS).astype(jnp.bfloat16)
    packed = got[:, ROBOTS:, :]
    seen = jnp.concatenate([packed[..., :COLS], packed[..., COLS:]], axis=1).reshape(TEAMS * ROBOTS, COLS)

    def one(a, b, left, right):
        return lax.dot_general(a, b, (((left,), (right,)), ((), ())), preferred_element_type=jnp.float32)

    first, second = split(seen)
    landmark = one(first, rows, 0, 0) + one(second, rows, 0, 0)
    first, second = split(landmark)
    back = (one(rows, first, 1, 1) + one(rows, second, 1, 1)).reshape(TEAMS, ROBOTS, COLS)
    part[..., :COLS] = back[:, : ROBOTS // 2, :]
    part[..., COLS:] = back[:, ROBOTS // 2 :, :]


def shards(transitions, states, cotangent, terminal, incidence, measured, obs_gain):
    matrix = transitions[0, 0]
    state = states[0, 0]
    cot = cotangent[0, 0]
    team = lax.axis_index("team")
    step = lax.axis_index("tm")
    even = team % 2 == 0
    ring = step // RING

    def pick(a, b):
        return jnp.where(even, a, b)

    other_matrix = send(matrix, TO_HOLDER)

    incident = incidence[0, 0].astype(jnp.float32)
    slices = incident.reshape(ROBOTS, TEAMS, LMK // TEAMS).transpose(1, 0, 2)
    packed = fold(measured[0, 0].T)
    packed = jnp.broadcast_to(packed[None], (TEAMS,) + packed.shape)
    got = lax.all_to_all(jnp.concatenate([slices, packed], axis=1), "team", 0, 0, tiled=True)
    part = pl.pallas_call(
        landmark_kernel,
        out_shape=jax.ShapeDtypeStruct((TEAMS, ROBOTS // 2, 2 * COLS), jnp.float32),
        name="landmark",
    )(got)
    parts = lax.all_to_all(part, "team", 0, 0, tiled=True)
    injected = jnp.sum(parts, axis=0)

    high = pick(other_matrix, matrix)
    low = pick(matrix, other_matrix)
    two = jnp.dot(high, low, precision=lax.Precision.HIGHEST)
    passing = send(two, LAST_STEP)
    two_far = send(two, FAR_IN)
    two_near = send(two, NEAR_IN)
    two_last = send(passing, FAR_IN)

    owner = jnp.arange(TEAM_STATES)[None, :] // STATES == jnp.arange(ROBOTS)[:, None]
    spread = lax.optimization_barrier(jnp.where(owner, obs_gain[0][None, :], 0.0))
    driven = cot + jnp.einsum("rc,rn->cn", unfold(injected), spread, precision=HIGH)
    other_driven = send(driven, OTHER_PAIRS)
    own_driven = send(driven, WORKER_PAIR)

    def compose_driven(other):
        later, sooner = pick(other, driven), pick(driven, other)
        return later, matmul(later, low) + sooner

    later, offset = compose_driven(other_driven)
    off_last = send(offset, LAST_IN)
    off_far = send(offset, FAR_IN)
    off_near = send(offset, NEAR_IN)

    own_later, own_offset = lax.optimization_barrier(compose_driven(own_driven))
    flag = even.astype(jnp.int32)[None]
    maps = (two, two_last, two_far, two_near)
    off3, shift1, shift0, total, leaving = sweep(
        flag, maps, (own_offset, off_last, off_far, off_near, terminal[0])
    )

    last_ring = STEPS // RING - 1
    incoming = send(leaving, ring_hop(last_ring))
    enter1, enter0, eight = compose(flag, maps, (shift1, shift0))
    map_near = send(enter0, NEAR_OUT)
    map_far = send(two, FAR_OUT_ODD)
    map_last = send(enter1, LAST_OUT_ODD)
    shift_far = send(off3, FAR_OUT)
    out = leaving
    for source in range(last_ring - 1, 0, -1):
        out = hop((ring == source).astype(jnp.int32)[None], incoming, eight, total, out)
        if source > 1:
            incoming = send(out, ring_hop(source))
    arrived = [
        send(out, down(last_pair)),
        send(out, down(near_pair)),
        send(out, down(far_pair)),
        send(out, down(own_pair)),
    ]
    pair = (step % RING) // 2

    def mine(rows, at_far):
        here = pick(enter1[rows], map_last[rows])
        return jnp.where(pair == NEAR, map_near[rows], jnp.where(pair == FAR, at_far, here))

    enter_map = mine(slice(0, TEAM_STATES), pick(passing, map_far))
    enter_shift = mine(slice(TEAM_STATES, None), shift_far)
    enter_map, enter_shift = lax.optimization_barrier((enter_map, enter_shift))
    entry = (arrived[0] + arrived[1]) + (arrived[2] + arrived[3]) + jnp.where(ring == last_ring, terminal[0], 0.0)
    entry = lax.optimization_barrier(entry)
    enter = jnp.where(pair == 3, entry, matmul(entry, enter_map) + enter_shift)
    enter = lax.optimization_barrier(enter)
    driven_high = jnp.where(pair == pick(own_pair(0), own_pair(1)), own_later, later)
    middle = matmul(enter, high) + driven_high
    passed = send(pick(enter, middle), TO_PARTNER)
    holds = step % 2 == team % 2
    running = jnp.where(holds, pick(middle, enter), passed)
    running = lax.optimization_barrier(running)
    grad = jnp.einsum("cn,cm->nm", running, state, precision=HIGH).astype(jnp.bfloat16)
    adjoint = matmul(running, matrix) + driven
    return adjoint[None, None], grad[None, None]


def solution(mesh):
    placed = (
        P("team", "tm", None, None),
        P("team", "tm", None, None),
        P("team", "tm", None, None),
        P("team", None, None),
        P("team", "tm", None, None),
        P("team", "tm", None, None),
        P("team", None),
    )
    return jax.shard_map(
        shards,
        mesh=mesh,
        in_specs=placed,
        out_specs=(P("team", "tm", None, None), P("team", "tm", None, None)),
        check_vma=False,
    )
```

```python
import jax
import jax.numpy as jnp
from jax import lax
from jax.experimental import pallas as pl
from jax.experimental.pallas import tpu as pltpu
from jax.sharding import PartitionSpec as P

STATES = 16
TEAM_STATES = 512
COLS = 64
ROBOTS = 32
LMK = 2048
TEAMS = 16
STEPS = 32
RING = 8
BOTH = ("team", "tm")

HIGH = lax.Precision.HIGH


def matmul(left, right):
    return jnp.dot(left, right, precision=HIGH)


def route(pairs_of):
    out = []
    for team in range(TEAMS):
        for ring in range(STEPS // RING):
            for src, dst in pairs_of(team % 2):
                base = team * STEPS + ring * RING
                out.append((base + src, base + dst))
    return out


def holder(pair, odd):
    return 2 * pair + odd


def partner(pair, odd):
    return 2 * pair + 1 - odd


NEAR = 0
FAR = 2


def own_pair(odd):
    return 3 if odd else 1


def last_pair(odd):
    return 1 if odd else 3


WORKER_PAIR = route(lambda odd: [(partner(own_pair(odd), odd), holder(own_pair(odd), odd))])
OTHER_PAIRS = route(
    lambda odd: [(partner(p, odd), holder(p, odd)) for p in range(4) if p != own_pair(odd)]
)
TO_HOLDER = route(lambda odd: [(partner(p, odd), holder(p, odd)) for p in range(4)])
TO_PARTNER = [(dst, src) for src, dst in TO_HOLDER]


def between(source, target, only_odd=False):
    def pairs_of(odd):
        if only_odd and not odd:
            return []
        return [(holder(source(odd), odd), holder(target(odd), odd))]

    return route(pairs_of)


def near_pair(odd):
    return NEAR


def far_pair(odd):
    return FAR


LAST_STEP = between(last_pair, far_pair)
FAR_IN = between(far_pair, own_pair)
NEAR_IN = between(near_pair, own_pair)
LAST_IN = between(last_pair, own_pair)
NEAR_OUT = between(own_pair, near_pair)
FAR_OUT = between(own_pair, far_pair)
FAR_OUT_ODD = between(own_pair, far_pair, True)
LAST_OUT_ODD = between(own_pair, last_pair, True)


def down(target):
    out = []
    for team in range(TEAMS):
        odd = team % 2
        for ring in range(1, STEPS // RING):
            base = team * STEPS + ring * RING
            out.append((base + holder(own_pair(odd), odd), base - RING + holder(target(odd), odd)))
    return out


def ring_hop(ring):
    out = []
    for team in range(TEAMS):
        z = holder(own_pair(team % 2), team % 2)
        out.append((team * STEPS + ring * RING + z, team * STEPS + (ring - 1) * RING + z))
    return out


def send(value, pairs):
    return lax.ppermute(value, BOTH, pairs)


def fold(rows):
    return jnp.concatenate([rows[..., :16, :], rows[..., 16:, :]], axis=-1)


def unfold(packed):
    return jnp.concatenate([packed[..., :64], packed[..., 64:]], axis=-2)


def split(value):
    high = value.astype(jnp.bfloat16)
    return high, (value - high.astype(jnp.float32)).astype(jnp.bfloat16)


def product(left, right, dims=(((1,), (0,)), ((), ()))):
    def one(a, b):
        return lax.dot_general(a, b, dims, preferred_element_type=jnp.float32)

    return one(left[0], right[0]) + (one(left[0], right[1]) + one(left[1], right[0]))


def copier(sems):
    return lambda src, dst, k: pltpu.make_async_copy(src, dst, sems.at[k])


def compose_kernel(
    flag, two, last, far, near, shift1, shift0, enter1, enter0, eight, m3, m2, m1, m0, r1, r0, r8, sems, out_sems
):
    load, store = copier(sems), copier(out_sems)
    even = flag[0] == 1

    @pl.when(even)
    def _():
        load(last, m3, 0).start()
        load(two, m1, 2).start()

    @pl.when(jnp.logical_not(even))
    def _():
        load(two, m3, 0).start()
        load(last, m1, 2).start()

    load(far, m2, 1).start()
    load(near, m0, 3).start()
    map_rows, shift_rows = pl.ds(0, TEAM_STATES), pl.ds(TEAM_STATES, COLS)
    store(shift1, enter1.at[shift_rows], 3).start()
    store(shift0, enter0.at[shift_rows], 4).start()
    load(last, m3, 0).wait()
    load(far, m2, 1).wait()
    r1[...] = product(split(m3[...]), split(m2[...]))
    store(r1, enter1.at[map_rows], 0).start()
    load(last, m1, 2).wait()
    r0[...] = product(split(r1[...]), split(m1[...]))
    store(r0, enter0.at[map_rows], 1).start()
    load(near, m0, 3).wait()
    r8[...] = product(split(r0[...]), split(m0[...]))
    store(r8, eight, 2).start()
    store(shift1, enter1.at[shift_rows], 3).wait()
    store(shift0, enter0.at[shift_rows], 4).wait()
    store(r1, enter1.at[map_rows], 0).wait()
    store(r0, enter0.at[map_rows], 1).wait()
    store(r8, eight, 2).wait()


SQUARE = (TEAM_STATES, TEAM_STATES)
ROWS = (COLS, TEAM_STATES)
TALL = (TEAM_STATES + COLS, TEAM_STATES)


def compose(flag, maps, shifts):
    return pl.pallas_call(
        compose_kernel,
        out_shape=[jax.ShapeDtypeStruct(shape, jnp.float32) for shape in (TALL, TALL, SQUARE)],
        in_specs=[pl.BlockSpec(memory_space=pltpu.SMEM)]
        + [pl.BlockSpec(memory_space=pl.ANY)] * 4
        + [pl.BlockSpec(memory_space=pltpu.VMEM)] * 2,
        out_specs=[pl.BlockSpec(memory_space=pl.ANY)] * 3,
        scratch_shapes=[pltpu.VMEM(SQUARE, jnp.float32)] * 7
        + [pltpu.SemaphoreType.DMA((4,)), pltpu.SemaphoreType.DMA((5,))],
        name="compose",
    )(flag, *maps, *shifts)


def sweep_kernel(
    flag, two, last, far, near, off_own, off_last, off_far, off_near, start,
    shift2, shift1, shift0, total, leaving, m3, m2, m1, m0, sems,
):
    load = copier(sems)
    even = flag[0] == 1

    @pl.when(even)
    def _():
        load(last, m3, 0).start()
        load(far, m2, 1).start()
        load(two, m1, 2).start()

    @pl.when(jnp.logical_not(even))
    def _():
        load(two, m3, 0).start()
        load(far, m2, 1).start()
        load(last, m1, 2).start()

    load(near, m0, 3).start()
    off3 = jnp.where(even, off_last[...], off_own[...])
    off1 = jnp.where(even, off_own[...], off_last[...])
    shift2[...] = off3
    load(last, m3, 0).wait()
    moved = product(split(start[...]), split(m3[...])) + off3
    both = jnp.concatenate([moved, off3], axis=0)

    def step(rows, weight, offset):
        return product(split(rows), split(weight)) + jnp.concatenate([offset, offset], axis=0)

    load(far, m2, 1).wait()
    both = step(both, m2[...], off_far[...])
    shift1[...] = both[COLS:]
    load(last, m1, 2).wait()
    both = step(both, m1[...], off1)
    shift0[...] = both[COLS:]
    load(near, m0, 3).wait()
    both = step(both, m0[...], off_near[...])
    total[...] = both[COLS:]
    leaving[...] = both[:COLS]


def sweep(flag, maps, rows):
    return pl.pallas_call(
        sweep_kernel,
        out_shape=[jax.ShapeDtypeStruct(ROWS, jnp.float32)] * 5,
        in_specs=[pl.BlockSpec(memory_space=pltpu.SMEM)]
        + [pl.BlockSpec(memory_space=pl.ANY)] * 4
        + [pl.BlockSpec(memory_space=pltpu.VMEM)] * 5,
        out_specs=[pl.BlockSpec(memory_space=pltpu.VMEM)] * 5,
        scratch_shapes=[pltpu.VMEM(SQUARE, jnp.float32)] * 4 + [pltpu.SemaphoreType.DMA((4,))],
        name="sweep",
    )(flag, *maps, *rows)


def hop_kernel(flag, arrived, eight, total, kept, out):
    @pl.when(flag[0] == 1)
    def _():
        out[...] = product(split(arrived[...]), split(eight[...])) + total[...]

    @pl.when(flag[0] == 0)
    def _():
        out[...] = kept[...]


def hop(flag, arrived, eight, total, kept):
    return pl.pallas_call(
        hop_kernel,
        out_shape=jax.ShapeDtypeStruct(ROWS, jnp.float32),
        in_specs=[pl.BlockSpec(memory_space=pltpu.SMEM)] + [pl.BlockSpec(memory_space=pltpu.VMEM)] * 4,
        out_specs=pl.BlockSpec(memory_space=pltpu.VMEM),
        name="hop",
    )(flag, arrived, eight, total, kept)


def enter_kernel(
    code, got0, got1, got2, got3, start, driven_high,
    near_map, far_pass, far_map, own_map, last_map, far_shift, matrix, other,
    passing, running, m, shift, mh, sems,
):
    load = copier(sems)
    role, is_last, even = code[0] % 8, (code[0] // 8) % 2 == 1, code[0] // 16 == 1
    map_rows, shift_rows = pl.ds(0, TEAM_STATES), pl.ds(TEAM_STATES, COLS)

    def fetch(table, offsets):
        load(table, m, 0).start()
        load(offsets, shift, 1).start()

    @pl.when(jnp.logical_or(role == 0, role == 4))
    def _():
        fetch(own_map.at[map_rows], own_map.at[shift_rows])

    @pl.when(role == 1)
    def _():
        fetch(near_map.at[map_rows], near_map.at[shift_rows])

    @pl.when(role == 2)
    def _():
        fetch(far_pass, far_shift)

    @pl.when(role == 3)
    def _():
        fetch(far_map, far_shift)

    @pl.when(role == 5)
    def _():
        fetch(last_map.at[map_rows], last_map.at[shift_rows])

    @pl.when(even)
    def _():
        load(other, mh, 2).start()

    @pl.when(jnp.logical_not(even))
    def _():
        load(matrix, mh, 2).start()

    entry = (got0[...] + got1[...]) + (got2[...] + got3[...]) + jnp.where(is_last, start[...], 0.0)
    load(far_pass, m, 0).wait()
    load(far_shift, shift, 1).wait()
    enter = jnp.where(role == 0, entry, product(split(entry), split(m[...])) + shift[...])
    load(other, mh, 2).wait()
    middle = product(split(enter), split(mh[...])) + driven_high[...]
    passing[...] = jnp.where(even, enter, middle)
    running[...] = jnp.where(even, middle, enter)


def enter_pair(code, rows, tables):
    return pl.pallas_call(
        enter_kernel,
        out_shape=[jax.ShapeDtypeStruct(ROWS, jnp.float32)] * 2,
        in_specs=[pl.BlockSpec(memory_space=pltpu.SMEM)]
        + [pl.BlockSpec(memory_space=pltpu.VMEM)] * 6
        + [pl.BlockSpec(memory_space=pl.ANY)] * 8,
        out_specs=[pl.BlockSpec(memory_space=pltpu.VMEM)] * 2,
        scratch_shapes=[
            pltpu.VMEM(SQUARE, jnp.float32),
            pltpu.VMEM(ROWS, jnp.float32),
            pltpu.VMEM(SQUARE, jnp.float32),
            pltpu.SemaphoreType.DMA((3,)),
        ],
        name="enter",
    )(code, *rows, *tables)


def landmark_kernel(got, part):
    rows = got[:, :ROBOTS, :].reshape(TEAMS * ROBOTS, LMK // TEAMS).astype(jnp.bfloat16)
    packed = got[:, ROBOTS:, :]
    seen = jnp.concatenate([packed[..., :COLS], packed[..., COLS:]], axis=1).reshape(TEAMS * ROBOTS, COLS)

    def one(a, b, left, right):
        return lax.dot_general(a, b, (((left,), (right,)), ((), ())), preferred_element_type=jnp.float32)

    first, second = split(seen)
    landmark = one(first, rows, 0, 0) + one(second, rows, 0, 0)
    first, second = split(landmark)
    back = (one(rows, first, 1, 1) + one(rows, second, 1, 1)).reshape(TEAMS, ROBOTS, COLS)
    part[..., :COLS] = back[:, : ROBOTS // 2, :]
    part[..., COLS:] = back[:, ROBOTS // 2 :, :]


def shards(transitions, states, cotangent, terminal, incidence, measured, obs_gain):
    matrix = transitions[0, 0]
    state = states[0, 0]
    cot = cotangent[0, 0]
    team = lax.axis_index("team")
    step = lax.axis_index("tm")
    even = team % 2 == 0
    ring = step // RING

    def pick(a, b):
        return jnp.where(even, a, b)

    other_matrix = send(matrix, TO_HOLDER)

    incident = incidence[0, 0].astype(jnp.float32)
    slices = incident.reshape(ROBOTS, TEAMS, LMK // TEAMS).transpose(1, 0, 2)
    packed = fold(measured[0, 0].T)
    packed = jnp.broadcast_to(packed[None], (TEAMS,) + packed.shape)
    got = lax.all_to_all(jnp.concatenate([slices, packed], axis=1), "team", 0, 0, tiled=True)
    part = pl.pallas_call(
        landmark_kernel,
        out_shape=jax.ShapeDtypeStruct((TEAMS, ROBOTS // 2, 2 * COLS), jnp.float32),
        name="landmark",
    )(got)
    parts = lax.all_to_all(part, "team", 0, 0, tiled=True)
    injected = jnp.sum(parts, axis=0)

    high = pick(other_matrix, matrix)
    low = pick(matrix, other_matrix)
    two = jnp.dot(high, low, precision=lax.Precision.HIGHEST)
    passing = send(two, LAST_STEP)
    two_far = send(two, FAR_IN)
    two_near = send(two, NEAR_IN)
    two_last = send(passing, FAR_IN)

    owner = jnp.arange(TEAM_STATES)[None, :] // STATES == jnp.arange(ROBOTS)[:, None]
    spread = lax.optimization_barrier(jnp.where(owner, obs_gain[0][None, :], 0.0))
    driven = cot + jnp.einsum("rc,rn->cn", unfold(injected), spread, precision=HIGH)
    other_driven = send(driven, OTHER_PAIRS)
    own_driven = send(driven, WORKER_PAIR)

    def compose_driven(other):
        later, sooner = pick(other, driven), pick(driven, other)
        return later, matmul(later, low) + sooner

    later, offset = compose_driven(other_driven)
    off_last = send(offset, LAST_IN)
    off_far = send(offset, FAR_IN)
    off_near = send(offset, NEAR_IN)

    own_later, own_offset = lax.optimization_barrier(compose_driven(own_driven))
    flag = even.astype(jnp.int32)[None]
    maps = (two, two_last, two_far, two_near)
    off3, shift1, shift0, total, leaving = sweep(
        flag, maps, (own_offset, off_last, off_far, off_near, terminal[0])
    )

    last_ring = STEPS // RING - 1
    incoming = send(leaving, ring_hop(last_ring))
    enter1, enter0, eight = compose(flag, maps, (shift1, shift0))
    map_near = send(enter0, NEAR_OUT)
    map_far = send(two, FAR_OUT_ODD)
    map_last = send(enter1, LAST_OUT_ODD)
    shift_far = send(off3, FAR_OUT)
    out = leaving
    for source in range(last_ring - 1, 0, -1):
        out = hop((ring == source).astype(jnp.int32)[None], incoming, eight, total, out)
        if source > 1:
            incoming = send(out, ring_hop(source))
    arrived = [
        send(out, down(last_pair)),
        send(out, down(near_pair)),
        send(out, down(far_pair)),
        send(out, down(own_pair)),
    ]
    pair = (step % RING) // 2
    is_own = pair == pick(own_pair(0), own_pair(1))
    driven_high = lax.optimization_barrier(jnp.where(is_own, own_later, later))
    role = jnp.where(pair == NEAR, 1, jnp.where(pair == FAR, pick(2, 3), jnp.where(pair == 3, 0, pick(4, 5))))
    code = role + 8 * (ring == last_ring).astype(jnp.int32) + 16 * even.astype(jnp.int32)
    passing_on, held = enter_pair(
        code.astype(jnp.int32)[None],
        (*arrived, terminal[0], driven_high),
        (map_near, passing, map_far, enter1, map_last, shift_far, matrix, other_matrix),
    )
    passed = send(passing_on, TO_PARTNER)
    holds = step % 2 == team % 2
    running = jnp.where(holds, held, passed)
    running = lax.optimization_barrier(running)
    grad = jnp.einsum("cn,cm->nm", running, state, precision=HIGH).astype(jnp.bfloat16)
    adjoint = matmul(running, matrix) + driven
    return adjoint[None, None], grad[None, None]


def solution(mesh):
    placed = (
        P("team", "tm", None, None),
        P("team", "tm", None, None),
        P("team", "tm", None, None),
        P("team", None, None),
        P("team", "tm", None, None),
        P("team", "tm", None, None),
        P("team", None),
    )
    return jax.shard_map(
        shards,
        mesh=mesh,
        in_specs=placed,
        out_specs=(P("team", "tm", None, None), P("team", "tm", None, None)),
        check_vma=False,
    )
```

```python
import jax
import jax.numpy as jnp
from jax import lax
from jax.experimental import pallas as pl
from jax.experimental.pallas import tpu as pltpu
from jax.sharding import PartitionSpec as P

STATES = 16
TEAM_STATES = 512
COLS = 64
ROBOTS = 32
LMK = 2048
TEAMS = 16
STEPS = 32
RING = 8
BOTH = ("team", "tm")

HIGH = lax.Precision.HIGH


def matmul(left, right):
    return jnp.dot(left, right, precision=HIGH)


def route(pairs_of):
    out = []
    for team in range(TEAMS):
        for ring in range(STEPS // RING):
            for src, dst in pairs_of(team % 2):
                base = team * STEPS + ring * RING
                out.append((base + src, base + dst))
    return out


def holder(pair, odd):
    return 2 * pair + odd


def partner(pair, odd):
    return 2 * pair + 1 - odd


NEAR = 0
FAR = 2


def own_pair(odd):
    return 3 if odd else 1


def last_pair(odd):
    return 1 if odd else 3


WORKER_PAIR = route(lambda odd: [(partner(own_pair(odd), odd), holder(own_pair(odd), odd))])
OTHER_PAIRS = route(
    lambda odd: [(partner(p, odd), holder(p, odd)) for p in range(4) if p != own_pair(odd)]
)
TO_HOLDER = route(lambda odd: [(partner(p, odd), holder(p, odd)) for p in range(4)])
TO_PARTNER = [(dst, src) for src, dst in TO_HOLDER]


def between(source, target, only_odd=False):
    def pairs_of(odd):
        if only_odd and not odd:
            return []
        return [(holder(source(odd), odd), holder(target(odd), odd))]

    return route(pairs_of)


def near_pair(odd):
    return NEAR


def far_pair(odd):
    return FAR


LAST_STEP = between(last_pair, far_pair)
FAR_IN = between(far_pair, own_pair)
NEAR_IN = between(near_pair, own_pair)
LAST_IN = between(last_pair, own_pair)
NEAR_OUT = between(own_pair, near_pair)
FAR_OUT = between(own_pair, far_pair)
FAR_OUT_ODD = between(own_pair, far_pair, True)
LAST_OUT_ODD = between(own_pair, last_pair, True)


def down(target):
    out = []
    for team in range(TEAMS):
        odd = team % 2
        for ring in range(1, STEPS // RING):
            base = team * STEPS + ring * RING
            out.append((base + holder(own_pair(odd), odd), base - RING + holder(target(odd), odd)))
    return out


def ring_hop(ring):
    out = []
    for team in range(TEAMS):
        z = holder(own_pair(team % 2), team % 2)
        out.append((team * STEPS + ring * RING + z, team * STEPS + (ring - 1) * RING + z))
    return out


def send(value, pairs):
    return lax.ppermute(value, BOTH, pairs)


def fold(rows):
    return jnp.concatenate([rows[..., :16, :], rows[..., 16:, :]], axis=-1)


def unfold(packed):
    return jnp.concatenate([packed[..., :64], packed[..., 64:]], axis=-2)


def split(value):
    high = value.astype(jnp.bfloat16)
    return high, (value - high.astype(jnp.float32)).astype(jnp.bfloat16)


def product(left, right, dims=(((1,), (0,)), ((), ()))):
    def one(a, b):
        return lax.dot_general(a, b, dims, preferred_element_type=jnp.float32)

    return one(left[0], right[0]) + (one(left[0], right[1]) + one(left[1], right[0]))


def copier(sems):
    return lambda src, dst, k: pltpu.make_async_copy(src, dst, sems.at[k])


HALF = TEAM_STATES // 2


def half_loads(load, parts, dst, k):
    tops = [load(part, dst.at[pl.ds(i * HALF, HALF)], k + i) for i, part in enumerate(parts)]
    return tops


def run(copies, wait=False):
    for copy in copies:
        if wait:
            copy.wait()
        else:
            copy.start()


def compose_kernel(
    flag, two, last_a, last_b, far, near, enter1, enter0, eight, m3, m2, m1, m0, r1, r0, r8, sems, out_sems
):
    load, store = copier(sems), copier(out_sems)
    even = flag[0] == 1
    last = (last_a, last_b)
    own = (two.at[pl.ds(0, HALF)], two.at[pl.ds(HALF, HALF)])

    @pl.when(even)
    def _():
        run(half_loads(load, last, m3, 0))
        run(half_loads(load, own, m1, 4))

    @pl.when(jnp.logical_not(even))
    def _():
        run(half_loads(load, own, m3, 0))
        run(half_loads(load, last, m1, 4))

    load(far, m2, 2).start()
    load(near, m0, 3).start()
    run(half_loads(load, last, m3, 0), True)
    load(far, m2, 2).wait()
    r1[...] = product(split(m3[...]), split(m2[...]))
    store(r1, enter1, 0).start()
    run(half_loads(load, last, m1, 4), True)
    r0[...] = product(split(r1[...]), split(m1[...]))
    store(r0, enter0, 1).start()
    load(near, m0, 3).wait()
    r8[...] = product(split(r0[...]), split(m0[...]))
    store(r8, eight, 2).start()
    store(r1, enter1, 0).wait()
    store(r0, enter0, 1).wait()
    store(r8, eight, 2).wait()


SQUARE = (TEAM_STATES, TEAM_STATES)
ROWS = (COLS, TEAM_STATES)


def compose(flag, two, last, far, near):
    return pl.pallas_call(
        compose_kernel,
        out_shape=[jax.ShapeDtypeStruct(SQUARE, jnp.float32)] * 3,
        in_specs=[pl.BlockSpec(memory_space=pltpu.SMEM)] + [pl.BlockSpec(memory_space=pl.ANY)] * 5,
        out_specs=[pl.BlockSpec(memory_space=pl.ANY)] * 3,
        scratch_shapes=[pltpu.VMEM(SQUARE, jnp.float32)] * 7
        + [pltpu.SemaphoreType.DMA((6,)), pltpu.SemaphoreType.DMA((3,))],
        name="compose",
    )(flag, two, *last, far, near)


def shift_kernel(
    flag, two, last_a, last_b, far, near, eight, off_own, off_last, off_far, off_near, start,
    shift2, shift1, shift0, total, leaving, m2, m1, m0, m8, sems,
):
    load = copier(sems)
    even = flag[0] == 1
    load(far, m2, 0).start()

    last = (last_a, last_b)
    own = (two.at[pl.ds(0, HALF)], two.at[pl.ds(HALF, HALF)])

    @pl.when(even)
    def _():
        run(half_loads(load, own, m1, 4))

    @pl.when(jnp.logical_not(even))
    def _():
        run(half_loads(load, last, m1, 4))

    load(near, m0, 2).start()
    load(eight, m8, 3).start()
    moved = jnp.where(even, off_last[...], off_own[...])
    off1 = jnp.where(even, off_own[...], off_last[...])
    shift2[...] = moved
    load(far, m2, 0).wait()
    moved = product(split(moved), split(m2[...])) + off_far[...]
    shift1[...] = moved
    run(half_loads(load, last, m1, 4), True)
    moved = product(split(moved), split(m1[...])) + off1
    shift0[...] = moved
    load(near, m0, 2).wait()
    moved = product(split(moved), split(m0[...])) + off_near[...]
    total[...] = moved
    load(eight, m8, 3).wait()
    leaving[...] = product(split(start[...]), split(m8[...])) + moved


def shift(flag, maps, rows):
    return pl.pallas_call(
        shift_kernel,
        out_shape=[jax.ShapeDtypeStruct(ROWS, jnp.float32)] * 5,
        in_specs=[pl.BlockSpec(memory_space=pltpu.SMEM)]
        + [pl.BlockSpec(memory_space=pl.ANY)] * 6
        + [pl.BlockSpec(memory_space=pltpu.VMEM)] * 5,
        out_specs=[pl.BlockSpec(memory_space=pltpu.VMEM)] * 5,
        scratch_shapes=[pltpu.VMEM(SQUARE, jnp.float32)] * 4 + [pltpu.SemaphoreType.DMA((6,))],
        name="shift",
    )(flag, *maps, *rows)


def hop_kernel(flag, arrived, eight, total, kept, out):
    @pl.when(flag[0] == 1)
    def _():
        out[...] = product(split(arrived[...]), split(eight[...])) + total[...]

    @pl.when(flag[0] == 0)
    def _():
        out[...] = kept[...]


def hop(flag, arrived, eight, total, kept):
    return pl.pallas_call(
        hop_kernel,
        out_shape=jax.ShapeDtypeStruct(ROWS, jnp.float32),
        in_specs=[pl.BlockSpec(memory_space=pltpu.SMEM)] + [pl.BlockSpec(memory_space=pltpu.VMEM)] * 4,
        out_specs=pl.BlockSpec(memory_space=pltpu.VMEM),
        name="hop",
    )(flag, arrived, eight, total, kept)


def landmark_kernel(got, part):
    rows = got[:, :ROBOTS, :].reshape(TEAMS * ROBOTS, LMK // TEAMS).astype(jnp.bfloat16)
    packed = got[:, ROBOTS:, :]
    seen = jnp.concatenate([packed[..., :COLS], packed[..., COLS:]], axis=1).reshape(TEAMS * ROBOTS, COLS)

    def one(a, b, left, right):
        return lax.dot_general(a, b, (((left,), (right,)), ((), ())), preferred_element_type=jnp.float32)

    first, second = split(seen)
    landmark = one(first, rows, 0, 0) + one(second, rows, 0, 0)
    first, second = split(landmark)
    back = (one(rows, first, 1, 1) + one(rows, second, 1, 1)).reshape(TEAMS, ROBOTS, COLS)
    part[..., :COLS] = back[:, : ROBOTS // 2, :]
    part[..., COLS:] = back[:, ROBOTS // 2 :, :]


def shards(transitions, states, cotangent, terminal, incidence, measured, obs_gain):
    matrix = transitions[0, 0]
    state = states[0, 0]
    cot = cotangent[0, 0]
    team = lax.axis_index("team")
    step = lax.axis_index("tm")
    even = team % 2 == 0
    ring = step // RING

    def pick(a, b):
        return jnp.where(even, a, b)

    other_matrix = send(matrix, TO_HOLDER)

    incident = incidence[0, 0].astype(jnp.float32)
    slices = incident.reshape(ROBOTS, TEAMS, LMK // TEAMS).transpose(1, 0, 2)
    packed = fold(measured[0, 0].T)
    packed = jnp.broadcast_to(packed[None], (TEAMS,) + packed.shape)
    got = lax.all_to_all(jnp.concatenate([slices, packed], axis=1), "team", 0, 0, tiled=True)
    part = pl.pallas_call(
        landmark_kernel,
        out_shape=jax.ShapeDtypeStruct((TEAMS, ROBOTS // 2, 2 * COLS), jnp.float32),
        name="landmark",
    )(got)
    parts = lax.all_to_all(part, "team", 0, 0, tiled=True)
    injected = jnp.sum(parts, axis=0)

    high = pick(other_matrix, matrix)
    low = pick(matrix, other_matrix)
    two = jnp.dot(high, low, precision=lax.Precision.HIGHEST)
    passing = [send(two[:HALF], LAST_STEP), send(two[HALF:], LAST_STEP)]
    two_far = send(two, FAR_IN)
    two_near = send(two, NEAR_IN)
    two_last = [send(passing[0], FAR_IN), send(passing[1], FAR_IN)]

    owner = jnp.arange(TEAM_STATES)[None, :] // STATES == jnp.arange(ROBOTS)[:, None]
    spread = lax.optimization_barrier(jnp.where(owner, obs_gain[0][None, :], 0.0))
    driven = cot + jnp.einsum("rc,rn->cn", unfold(injected), spread, precision=HIGH)
    other_driven = send(driven, OTHER_PAIRS)
    own_driven = send(driven, WORKER_PAIR)

    def compose_driven(other):
        later, sooner = pick(other, driven), pick(driven, other)
        return later, matmul(later, low) + sooner

    later, offset = compose_driven(other_driven)
    off_last = send(offset, LAST_IN)
    off_far = send(offset, FAR_IN)
    off_near = send(offset, NEAR_IN)

    own_later, own_offset = lax.optimization_barrier(compose_driven(own_driven))
    flag = even.astype(jnp.int32)[None]
    enter1, enter0, eight = compose(flag, two, two_last, two_far, two_near)
    off3, shift1, shift0, total, leaving = shift(
        flag,
        (two, *two_last, two_far, two_near, eight),
        (own_offset, off_last, off_far, off_near, terminal[0]),
    )

    last_ring = STEPS // RING - 1
    incoming = send(leaving, ring_hop(last_ring))
    map_near = send(enter0, NEAR_OUT)
    map_far = send(two, FAR_OUT_ODD)
    map_last = send(enter1, LAST_OUT_ODD)
    shift_near = send(shift0, NEAR_OUT)
    shift_far = send(off3, FAR_OUT)
    shift_last = send(shift1, LAST_OUT_ODD)
    out = leaving
    for source in range(last_ring - 1, 0, -1):
        out = hop((ring == source).astype(jnp.int32)[None], incoming, eight, total, out)
        if source > 1:
            incoming = send(out, ring_hop(source))
    arrived = [
        send(out, down(last_pair)),
        send(out, down(near_pair)),
        send(out, down(far_pair)),
        send(out, down(own_pair)),
    ]
    pair = (step % RING) // 2
    enter_map = jnp.where(pair == NEAR, map_near, jnp.where(pair == FAR, pick(jnp.concatenate(passing, axis=0), map_far), pick(enter1, map_last)))
    enter_shift = jnp.where(pair == NEAR, shift_near, jnp.where(pair == FAR, shift_far, pick(shift1, shift_last)))
    enter_map, enter_shift = lax.optimization_barrier((enter_map, enter_shift))
    entry = (arrived[0] + arrived[1]) + (arrived[2] + arrived[3]) + jnp.where(ring == last_ring, terminal[0], 0.0)
    entry = lax.optimization_barrier(entry)
    enter = jnp.where(pair == 3, entry, matmul(entry, enter_map) + enter_shift)
    enter = lax.optimization_barrier(enter)
    driven_high = jnp.where(pair == pick(own_pair(0), own_pair(1)), own_later, later)
    middle = matmul(enter, high) + driven_high
    passed = send(pick(enter, middle), TO_PARTNER)
    holds = step % 2 == team % 2
    running = jnp.where(holds, pick(middle, enter), passed)
    running = lax.optimization_barrier(running)
    grad = jnp.einsum("cn,cm->nm", running, state, precision=HIGH).astype(jnp.bfloat16)
    adjoint = matmul(running, matrix) + driven
    return adjoint[None, None], grad[None, None]


def solution(mesh):
    placed = (
        P("team", "tm", None, None),
        P("team", "tm", None, None),
        P("team", "tm", None, None),
        P("team", None, None),
        P("team", "tm", None, None),
        P("team", "tm", None, None),
        P("team", None),
    )
    return jax.shard_map(
        shards,
        mesh=mesh,
        in_specs=placed,
        out_specs=(P("team", "tm", None, None), P("team", "tm", None, None)),
        check_vma=False,
    )
```

```python
import jax
import jax.numpy as jnp
from jax import lax
from jax.experimental import pallas as pl
from jax.experimental.pallas import tpu as pltpu
from jax.sharding import PartitionSpec as P

STATES = 16
TEAM_STATES = 512
COLS = 64
ROBOTS = 32
LMK = 2048
TEAMS = 16
STEPS = 32
RING = 8
BOTH = ("team", "tm")

HIGH = lax.Precision.HIGH


def matmul(left, right):
    return jnp.dot(left, right, precision=HIGH)


def route(pairs_of):
    out = []
    for team in range(TEAMS):
        for ring in range(STEPS // RING):
            for src, dst in pairs_of(team % 2):
                base = team * STEPS + ring * RING
                out.append((base + src, base + dst))
    return out


def holder(pair, odd):
    return 2 * pair + odd


def partner(pair, odd):
    return 2 * pair + 1 - odd


NEAR = 0
FAR = 2


def own_pair(odd):
    return 3 if odd else 1


def last_pair(odd):
    return 1 if odd else 3


WORKER_PAIR = route(lambda odd: [(partner(own_pair(odd), odd), holder(own_pair(odd), odd))])
OTHER_PAIRS = route(
    lambda odd: [(partner(p, odd), holder(p, odd)) for p in range(4) if p != own_pair(odd)]
)
TO_HOLDER = route(lambda odd: [(partner(p, odd), holder(p, odd)) for p in range(4)])
TO_PARTNER = [(dst, src) for src, dst in TO_HOLDER]


def between(source, target, only_odd=False):
    def pairs_of(odd):
        if only_odd and not odd:
            return []
        return [(holder(source(odd), odd), holder(target(odd), odd))]

    return route(pairs_of)


def near_pair(odd):
    return NEAR


def far_pair(odd):
    return FAR


LAST_STEP = between(last_pair, far_pair)
FAR_IN = between(far_pair, own_pair)
NEAR_IN = between(near_pair, own_pair)
LAST_IN = between(last_pair, own_pair)
NEAR_OUT = between(own_pair, near_pair)
FAR_OUT = between(own_pair, far_pair)
FAR_OUT_ODD = between(own_pair, far_pair, True)
LAST_OUT_ODD = between(own_pair, last_pair, True)


def down(target):
    out = []
    for team in range(TEAMS):
        odd = team % 2
        for ring in range(1, STEPS // RING):
            base = team * STEPS + ring * RING
            out.append((base + holder(own_pair(odd), odd), base - RING + holder(target(odd), odd)))
    return out


def ring_hop(ring):
    out = []
    for team in range(TEAMS):
        z = holder(own_pair(team % 2), team % 2)
        out.append((team * STEPS + ring * RING + z, team * STEPS + (ring - 1) * RING + z))
    return out


def send(value, pairs):
    return lax.ppermute(value, BOTH, pairs)


def fold(rows):
    return jnp.concatenate([rows[..., :16, :], rows[..., 16:, :]], axis=-1)


def unfold(packed):
    return jnp.concatenate([packed[..., :64], packed[..., 64:]], axis=-2)


def split(value):
    high = value.astype(jnp.bfloat16)
    return high, (value - high.astype(jnp.float32)).astype(jnp.bfloat16)


def product(left, right, dims=(((1,), (0,)), ((), ()))):
    def one(a, b):
        return lax.dot_general(a, b, dims, preferred_element_type=jnp.float32)

    return one(left[0], right[0]) + (one(left[0], right[1]) + one(left[1], right[0]))


def compose_kernel(
    flag, two, last, far, near, off_own, off_last, off_far, off_near, start,
    enter1, enter0, eight, shift1, shift0, total, leaving,
    m3, m2, m1, m0, r1, r0, r8, sems, out_sems,
):
    def load(src, dst, k):
        return pltpu.make_async_copy(src, dst, sems.at[k])

    def store(src, dst, k):
        return pltpu.make_async_copy(src, dst, out_sems.at[k])

    even = flag[0] == 1

    @pl.when(even)
    def _():
        load(last, m3, 0).start()
        load(two, m1, 2).start()

    @pl.when(jnp.logical_not(even))
    def _():
        load(two, m3, 0).start()
        load(last, m1, 2).start()

    load(far, m2, 1).start()
    load(near, m0, 3).start()
    off3 = jnp.where(even, off_last[...], off_own[...])
    off1 = jnp.where(even, off_own[...], off_last[...])
    load(last, m3, 0).wait()
    load(far, m2, 1).wait()
    weight = split(m2[...])
    r1[...] = product(split(m3[...]), weight)
    store(r1, enter1, 0).start()
    moved = product(split(off3), weight) + off_far[...]
    shift1[...] = moved
    load(last, m1, 2).wait()
    weight = split(m1[...])
    r0[...] = product(split(r1[...]), weight)
    store(r0, enter0, 1).start()
    moved = product(split(moved), weight) + off1
    shift0[...] = moved
    load(near, m0, 3).wait()
    weight = split(m0[...])
    r8[...] = product(split(r0[...]), weight)
    store(r8, eight, 2).start()
    moved = product(split(moved), weight) + off_near[...]
    total[...] = moved
    leaving[...] = product(split(start[...]), split(r8[...])) + moved
    store(r1, enter1, 0).wait()
    store(r0, enter0, 1).wait()
    store(r8, eight, 2).wait()


def compose(even, maps, rows):
    shape = (TEAM_STATES, TEAM_STATES)
    small = (COLS, TEAM_STATES)
    spaces = [pl.BlockSpec(memory_space=pl.ANY)] * 4 + [pl.BlockSpec(memory_space=pltpu.VMEM)] * 5
    return pl.pallas_call(
        compose_kernel,
        out_shape=[jax.ShapeDtypeStruct(shape, jnp.float32)] * 3 + [jax.ShapeDtypeStruct(small, jnp.float32)] * 4,
        in_specs=[pl.BlockSpec(memory_space=pltpu.SMEM)] + spaces,
        out_specs=[pl.BlockSpec(memory_space=pl.ANY)] * 3 + [pl.BlockSpec(memory_space=pltpu.VMEM)] * 4,
        scratch_shapes=[pltpu.VMEM(shape, jnp.float32)] * 7
        + [pltpu.SemaphoreType.DMA((4,)), pltpu.SemaphoreType.DMA((3,))],
        name="compose",
    )(even.astype(jnp.int32)[None], *maps, *rows)


def landmark_kernel(got, part):
    rows = got[:, :ROBOTS, :].reshape(TEAMS * ROBOTS, LMK // TEAMS).astype(jnp.bfloat16)
    packed = got[:, ROBOTS:, :]
    seen = jnp.concatenate([packed[..., :COLS], packed[..., COLS:]], axis=1).reshape(TEAMS * ROBOTS, COLS)

    def one(a, b, left, right):
        return lax.dot_general(a, b, (((left,), (right,)), ((), ())), preferred_element_type=jnp.float32)

    first, second = split(seen)
    landmark = one(first, rows, 0, 0) + one(second, rows, 0, 0)
    first, second = split(landmark)
    back = (one(rows, first, 1, 1) + one(rows, second, 1, 1)).reshape(TEAMS, ROBOTS, COLS)
    part[..., :COLS] = back[:, : ROBOTS // 2, :]
    part[..., COLS:] = back[:, ROBOTS // 2 :, :]


def shards(transitions, states, cotangent, terminal, incidence, measured, obs_gain):
    matrix = transitions[0, 0]
    state = states[0, 0]
    cot = cotangent[0, 0]
    team = lax.axis_index("team")
    step = lax.axis_index("tm")
    even = team % 2 == 0
    ring = step // RING

    def pick(a, b):
        return jnp.where(even, a, b)

    other_matrix = send(matrix, TO_HOLDER)

    incident = incidence[0, 0].astype(jnp.float32)
    slices = incident.reshape(ROBOTS, TEAMS, LMK // TEAMS).transpose(1, 0, 2)
    packed = fold(measured[0, 0].T)
    packed = jnp.broadcast_to(packed[None], (TEAMS,) + packed.shape)
    got = lax.all_to_all(jnp.concatenate([slices, packed], axis=1), "team", 0, 0, tiled=True)
    part = pl.pallas_call(
        landmark_kernel,
        out_shape=jax.ShapeDtypeStruct((TEAMS, ROBOTS // 2, 2 * COLS), jnp.float32),
        name="landmark",
    )(got)
    parts = lax.all_to_all(part, "team", 0, 0, tiled=True)
    injected = jnp.sum(parts, axis=0)

    high = pick(other_matrix, matrix)
    low = pick(matrix, other_matrix)
    two = jnp.dot(high, low, precision=lax.Precision.HIGHEST)
    passing = send(two, LAST_STEP)
    two_far = send(two, FAR_IN)
    two_near = send(two, NEAR_IN)
    two_last = send(passing, FAR_IN)

    owner = jnp.arange(TEAM_STATES)[None, :] // STATES == jnp.arange(ROBOTS)[:, None]
    spread = lax.optimization_barrier(jnp.where(owner, obs_gain[0][None, :], 0.0))
    driven = cot + jnp.einsum("rc,rn->cn", unfold(injected), spread, precision=HIGH)
    other_driven = send(driven, OTHER_PAIRS)
    own_driven = send(driven, WORKER_PAIR)

    def compose_driven(other):
        later, sooner = pick(other, driven), pick(driven, other)
        return later, matmul(later, low) + sooner

    later, offset = compose_driven(other_driven)
    off_last = send(offset, LAST_IN)
    off_far = send(offset, FAR_IN)
    off_near = send(offset, NEAR_IN)

    own_later, own_offset = lax.optimization_barrier(compose_driven(own_driven))
    enter1, enter0, eight, shift1, shift0, total, leaving = compose(
        even, (two, two_last, two_far, two_near), (own_offset, off_last, off_far, off_near, terminal[0])
    )
    off3 = pick(off_last, own_offset)

    last_ring = STEPS // RING - 1
    incoming = send(leaving, ring_hop(last_ring))
    map_near = send(enter0, NEAR_OUT)
    map_far = send(two, FAR_OUT_ODD)
    map_last = send(enter1, LAST_OUT_ODD)
    shift_near = send(shift0, NEAR_OUT)
    shift_far = send(off3, FAR_OUT)
    shift_last = send(shift1, LAST_OUT_ODD)
    out = leaving
    for source in range(last_ring - 1, 0, -1):
        leaving = matmul(incoming, eight) + total
        out = jnp.where(ring == source, leaving, out)
        if source > 1:
            incoming = send(leaving, ring_hop(source))
    arrived = [
        send(out, down(last_pair)), send(out, down(near_pair)), send(out, down(far_pair)), send(out, down(own_pair))
    ]
    pair = (step % RING) // 2
    enter_map = jnp.where(pair == NEAR, map_near, jnp.where(pair == FAR, pick(passing, map_far), pick(enter1, map_last)))
    enter_shift = jnp.where(pair == NEAR, shift_near, jnp.where(pair == FAR, shift_far, pick(shift1, shift_last)))
    enter_map, enter_shift = lax.optimization_barrier((enter_map, enter_shift))
    entry = (arrived[0] + arrived[1]) + (arrived[2] + arrived[3]) + jnp.where(ring == last_ring, terminal[0], 0.0)
    entry = lax.optimization_barrier(entry)
    enter = jnp.where(pair == 3, entry, matmul(entry, enter_map) + enter_shift)
    enter = lax.optimization_barrier(enter)
    driven_high = jnp.where(pair == pick(own_pair(0), own_pair(1)), own_later, later)
    middle = matmul(enter, high) + driven_high
    passed = send(pick(enter, middle), TO_PARTNER)
    holds = step % 2 == team % 2
    running = jnp.where(holds, pick(middle, enter), passed)
    running = lax.optimization_barrier(running)
    grad = jnp.einsum("cn,cm->nm", running, state, precision=HIGH).astype(jnp.bfloat16)
    adjoint = matmul(running, matrix) + driven
    return adjoint[None, None], grad[None, None]


def solution(mesh):
    placed = (
        P("team", "tm", None, None),
        P("team", "tm", None, None),
        P("team", "tm", None, None),
        P("team", None, None),
        P("team", "tm", None, None),
        P("team", "tm", None, None),
        P("team", None),
    )
    return jax.shard_map(
        shards,
        mesh=mesh,
        in_specs=placed,
        out_specs=(P("team", "tm", None, None), P("team", "tm", None, None)),
        check_vma=False,
    )
```
